32 devices in a mesh: gx: 8 (over z, core), gy: 4 (over y, x).
Axes of the slice: x: 2, y: 2, z: 4, core: 2. Of those that a mesh axis runs over, the one named last changes fastest.
Arguments:
- key_rows: bfloat16 [16384, 3072], P(('gx', 'gy')), may hold values from -6 to 6
- value_rows: bfloat16 [16384, 3072], P(('gx', 'gy')), may hold values from -6 to 6
- query_rows: bfloat16 [16384, 3072], P(('gx', 'gy')), may hold values from -6 to 6
- token_rates: float32 [16384, 48], P(('gx', 'gy')), may hold values from 0.1 to 1
- fast_weights: float32 [3072, 512], P(('gx', 'gy')), may hold values from -0.6 to 0.6
- momentum: float32 [3072, 512], P(('gx', 'gy')), may hold values from -0.3 to 0.3
- norm_gain: float32 [48, 64], replicated, may hold values from 0.5 to 1.5
- norm_bias: float32 [48, 64], replicated, may hold values from -1.5 to 1.5
Outputs:
- mixed: bfloat16 [16384, 3072], P(('gx', 'gy'))
- new_fast: float32 [3072, 512], P(('gx', 'gy'))
- new_moment: float32 [3072, 512], P(('gx', 'gy'))
The draws below stay inside these ranges and needn't reach their ends.
All inputs are finite; a program needn't handle non-finite values.
Results may differ from the reference program's by a relative error of at most 0.0095.
Values may be sent and summed in bfloat16 or wider, within the bound.
No kernel may reach another device: no remote copies, remote signals or barrier semaphores. Data moves between devices by JAX's collectives and lax.ppermute only.
A program may use at most 128 MiB of HBM per device.

```python
import math
import jax
import jax.numpy as jnp
from jax import lax

H = 48
HD = 64
FH = 256
STEPS = 2
TOK_DEV = 512
D = 3072
TOKENS = 16384
DEVICES = 32


def strengthened(drawn, rng, source, target, blocks, factor):
    owner, partner = [(jnp.arange(drawn.shape[axis_at]) // (drawn.shape[axis_at] // blocks)).reshape([-1 if axis == axis_at else 1 for axis in range(drawn.ndim)]) for axis_at in (source, target)]
    chosen = jax.random.permutation(rng, blocks)[partner]
    strong = (owner == chosen) | (owner == (partner + blocks // 2) % blocks)
    return jnp.where(strong, factor * drawn, drawn)


def shard_levels(rng, dims, shards, low, top_value):
    level = 1.0
    for position, shards_of in shards:
        draws = jax.random.uniform(jax.random.fold_in(jax.random.fold_in(rng, 6), position), (shards_of,), jnp.float32, low / len(shards), top_value / len(shards))
        level = level * jnp.repeat(jnp.exp(draws), dims[position] // shards_of).reshape((-1,) + (1,) * (len(dims) - 1 - position))
    return level


def centred(rng, dims, scale, bound, cuts=(), held_as=jnp.bfloat16):
    drawn = scale * jax.random.normal(rng, dims, jnp.float32)
    if cuts:
        drawn = drawn * shard_levels(rng, dims, cuts, -0.22, 0.18)
    return jnp.clip(drawn, -bound, bound).astype(held_as)


def noise_with(rng, extent, scale, most, pieces, heavy, kind=jnp.bfloat16):
    values = scale * jax.random.normal(rng, extent, jnp.float32)
    if pieces:
        values = values * shard_levels(rng, extent, pieces, -0.22, 0.18)
    return jnp.clip(strengthened(values, jax.random.fold_in(rng, 3), *heavy), -most, most).astype(kind)


def setup_inputs(seed: int = 0) -> dict:
    keys = jax.random.split(jax.random.key(seed), 9)
    key_rows = noise_with(keys[0], (TOKENS, D), 1.0, 6.0, ((0, 32),), (0, 1, 32, 2.75))
    value_rows = centred(keys[1], (TOKENS, D), 1.0, 6.0, ((0, 32),))
    query_rows = centred(keys[2], (TOKENS, D), 1.0, 6.0, ((0, 32),))
    token_rates = jnp.clip(jnp.exp(math.log(1.0) - 2.3025851 * jax.random.uniform(keys[3], (TOKENS, H), jnp.float32) ** shard_levels(keys[3], (TOKENS, H), ((0, 32),), -0.2, 0.2)), 0.1, 1.0)
    fast_weights = centred(keys[4], (D, 2 * FH), 0.1, 0.6, ((0, 32),), jnp.float32)
    momentum = centred(keys[5], (D, 2 * FH), 0.05, 0.3, ((0, 32),), jnp.float32)
    norm_gain = jnp.clip(1.0 + 0.1 * jax.random.normal(keys[6], (H, HD), jnp.float32), 0.5, 1.5)
    norm_bias = centred(keys[7], (H, HD), 0.3, 1.5, (), jnp.float32)
    return {"key_rows": key_rows, "value_rows": value_rows, "query_rows": query_rows, "token_rates": token_rates, "fast_weights": fast_weights, "momentum": momentum, "norm_gain": norm_gain, "norm_bias": norm_bias}


momentum_keep = 0.9
inner_rate = 0.5

def normalize(hidden, gain, bias):
    centre = hidden - lax.optimization_barrier(jnp.mean(hidden, axis=-1, keepdims=True))
    spread = lax.optimization_barrier(jnp.mean(centre * centre, axis=-1, keepdims=True))
    return centre * lax.rsqrt(spread + 1e-06) * gain + bias

def predict(inputs, packed, gain, bias):
    width = packed.shape[-1] // 2
    first = jnp.einsum('tgd,gdf->tgf', inputs, packed[:, :, :width])
    active = jax.nn.gelu(first)
    second = jnp.einsum('tgf,gdf->tgd', active, packed[:, :, width:])
    return normalize(second, gain, bias)

def grouped(array, heads):
    return jnp.moveaxis(array.reshape(array.shape[0], heads // 2, 2, -1), 1, 0)

def shard_gradient(key_rows, value_rows, token_rates, weights, gain, bias, total):
    heads = token_rates.shape[1]
    inputs = grouped(key_rows.astype(jnp.float32), heads)
    targets = grouped(value_rows.astype(jnp.float32), heads) - inputs
    rates = jnp.moveaxis(token_rates.reshape(token_rates.shape[0], heads // 2, 2), 1, 0)
    packed = weights.reshape(heads // 2, 2, -1, weights.shape[1])
    gains = gain.reshape(heads // 2, 2, -1)
    biases = bias.reshape(heads // 2, 2, -1)

    def per_group(items):
        inputs_g, targets_g, rates_g, packed_g, gain_g, bias_g = items

        def loss(packed_now):
            error = predict(inputs_g, packed_now, gain_g, bias_g) - targets_g
            return 0.5 * jnp.sum(rates_g[..., None] * error * error) / total
        return jax.grad(loss)(packed_g)
    grads = lax.map(per_group, (inputs, targets, rates, packed, gains, biases))
    return grads.reshape(weights.shape)

def shard_output(query_rows, weights, gain, bias):
    heads = gain.shape[0]
    inputs = grouped(query_rows.astype(jnp.float32), heads)
    packed = weights.reshape(heads // 2, 2, -1, weights.shape[1])
    gains = gain.reshape(heads // 2, 2, -1)
    biases = bias.reshape(heads // 2, 2, -1)

    def per_group(items):
        return predict(items[0], items[1], items[2], items[3])
    outputs = lax.map(per_group, (inputs, packed, gains, biases))
    outputs = jnp.moveaxis(outputs, 0, 1).reshape(query_rows.shape)
    return (query_rows.astype(jnp.float32) + outputs).astype(jnp.bfloat16)

def rounded(array):
    return lax.optimization_barrier(array.astype(jnp.bfloat16)).astype(array.dtype)

def split_rows(array):
    return array.reshape(DEVICES, TOK_DEV, array.shape[1])

def reference(key_rows, value_rows, query_rows, token_rates, fast_weights, momentum, norm_gain, norm_bias):
    fast, moment = (fast_weights, momentum)
    for step in range(STEPS):
        weights = rounded(fast)

        def add_shard(carry, items):
            part = shard_gradient(items[0], items[1], items[2], weights, norm_gain, norm_bias, TOKENS)
            return (carry + rounded(part), None)
        grad, unused = lax.scan(add_shard, jnp.zeros_like(fast), (split_rows(key_rows), split_rows(value_rows), split_rows(token_rates)))
        moment = momentum_keep * moment + grad
        fast = fast - inner_rate * moment
    weights = rounded(fast)

    def apply_shard(queries):
        return shard_output(queries, weights, norm_gain, norm_bias)
    mixed = lax.map(apply_shard, split_rows(query_rows)).reshape(TOKENS, D)
    return (mixed, fast, moment)
```

```python
import functools
import jax
import jax.numpy as jnp
from jax import lax
from jax.experimental import pallas as pl
from jax.experimental.pallas import tpu as pltpu

from jax.sharding import PartitionSpec as P

STEPS = 2

momentum_keep = 0.9
inner_rate = 0.5

KIND = jnp.float32
GELU_SCALE = 0.7978845608028654
GELU_CUBIC = 0.044715
NT = (((1,), (1,)), ((), ()))
NN = (((1,), (0,)), ((), ()))

def dot(a, b, dims=NN):
    return lax.dot_general(a, b, dims, preferred_element_type=jnp.float32)

def blocks(packed, size):
    width = packed.shape[1] // 2
    top, low = packed[:size], packed[size:]
    def diag(a, b):
        a = jnp.concatenate([a, jnp.zeros_like(a)], axis=1)
        b = jnp.concatenate([jnp.zeros_like(b), b], axis=1)
        return jnp.concatenate([a, b], axis=0).astype(jnp.bfloat16)
    def centred(a):
        a = a[:, width:].astype(jnp.float32)
        return a - jnp.mean(a, axis=0, keepdims=True)
    return diag(top[:, :width], low[:, :width]), diag(centred(top), centred(low))

def pair_mean(size):
    row = lax.broadcasted_iota(jnp.int32, (2 * size, 2 * size), 0) // size
    col = lax.broadcasted_iota(jnp.int32, (2 * size, 2 * size), 1) // size
    return jnp.where(row == col, 1.0 / size, 0.0).astype(jnp.bfloat16)

def activate(first, grad, kind):
    first = first.astype(kind)
    square = first * first
    inner = first * (square * jnp.asarray(GELU_SCALE * GELU_CUBIC, kind) + jnp.asarray(GELU_SCALE, kind))
    half = jnp.tanh(inner) * jnp.asarray(0.5, kind) + jnp.asarray(0.5, kind)
    active = first * half
    if not grad:
        return active.astype(jnp.bfloat16), None
    poly = square * jnp.asarray(6 * GELU_SCALE * GELU_CUBIC, kind) + jnp.asarray(2 * GELU_SCALE, kind)
    slope = half + active * (jnp.asarray(1.0, kind) - half) * poly
    return active.astype(jnp.bfloat16), slope

def grad_kernel(size, chunk, total, kind, key_ref, value_ref, rate_ref, packed_ref, gain_ref, bias_ref, out_ref,
                active_ref, dfirst_ref, dsecond_ref):
    tokens = key_ref.shape[0]
    width = packed_ref.shape[1] // 2
    first_w, second_w = blocks(packed_ref[...], size)
    mean = pair_mean(size)
    gain = gain_ref[0]
    bias = bias_ref[0]
    scaled = gain * (1.0 / total)
    for at in range(0, tokens, chunk):
        rows = pl.ds(at, chunk)
        keys = key_ref[rows, :]
        first = dot(keys, first_w)
        active, slope = activate(first, True, kind)
        active_ref[rows, :] = active
        centre = dot(active, second_w, NT)
        spread = dot((centre * centre).astype(jnp.bfloat16), mean)
        inverse = lax.rsqrt(spread + 1e-06)
        unit = centre * inverse
        target = value_ref[rows, :].astype(jnp.float32) - keys.astype(jnp.float32)
        error = unit * gain + (bias - target)
        dunit = error * (rate_ref[rows, :].astype(jnp.float32) * scaled)
        along = dot((dunit * unit).astype(jnp.bfloat16), mean)
        dsecond = (inverse * (dunit - unit * along)).astype(jnp.bfloat16)
        dsecond_ref[rows, :] = dsecond
        dactive = dot(dsecond, second_w)
        dfirst_ref[rows, :] = (dactive.astype(kind) * slope).astype(jnp.bfloat16)
    keys_t = key_ref[...].T
    dsecond_t = dsecond_ref[...].T
    for head in range(2):
        mine = slice(head * size, (head + 1) * size)
        cols = slice(head * width, (head + 1) * width)
        out_ref[mine, :width] = dot(keys_t[mine], dfirst_ref[:, cols]).astype(out_ref.dtype)
        second = dot(dsecond_t[mine], active_ref[:, cols])
        out_ref[mine, width:] = (second - jnp.mean(second, axis=0, keepdims=True)).astype(out_ref.dtype)

def apply_kernel(size, chunk, kind, query_ref, packed_ref, gain_ref, bias_ref, out_ref):
    tokens = query_ref.shape[0]
    first_w, second_w = blocks(packed_ref[...], size)
    mean = pair_mean(size)
    gain = gain_ref[0]
    bias = bias_ref[0]
    for at in range(0, tokens, chunk):
        rows = pl.ds(at, chunk)
        queries = query_ref[rows, :]
        first = dot(queries, first_w)
        active, _ = activate(first, False, kind)
        centre = dot(active, second_w, NT)
        spread = dot((centre * centre).astype(jnp.bfloat16), mean)
        unit = centre * lax.rsqrt(spread + 1e-06)
        out_ref[rows, :] = (queries.astype(jnp.float32) + unit * gain + bias).astype(out_ref.dtype)

def gradient(keys, values, rates, packed, gain, bias, total, size, chunk=128, kind=jnp.float32):
    tokens = keys.shape[0]
    rows, two = packed.shape
    pairs = rows // (2 * size)
    col = pl.BlockSpec((tokens, 2 * size), lambda i: (0, i))
    vec = pl.BlockSpec((1, 1, 2 * size), lambda i: (i, 0, 0))
    mat = pl.BlockSpec((2 * size, two), lambda i: (i, 0))
    return pl.pallas_call(
        functools.partial(grad_kernel, size, chunk, total, kind),
        out_shape=jax.ShapeDtypeStruct((rows, two), jnp.bfloat16),
        grid=(pairs,),
        in_specs=[col, col, col, mat, vec, vec],
        out_specs=mat,
        scratch_shapes=[pltpu.VMEM((tokens, two), jnp.bfloat16), pltpu.VMEM((tokens, two), jnp.bfloat16), pltpu.VMEM((tokens, 2 * size), jnp.bfloat16)],
        name="fast_gradient",
    )(keys, values, rates, packed, gain.reshape(pairs, 1, 2 * size), bias.reshape(pairs, 1, 2 * size))

def output(queries, packed, gain, bias, size, chunk=128, kind=jnp.float32):
    tokens = queries.shape[0]
    rows, two = packed.shape
    pairs = rows // (2 * size)
    col = pl.BlockSpec((tokens, 2 * size), lambda i: (0, i))
    vec = pl.BlockSpec((1, 1, 2 * size), lambda i: (i, 0, 0))
    mat = pl.BlockSpec((2 * size, two), lambda i: (i, 0))
    return pl.pallas_call(
        functools.partial(apply_kernel, size, chunk, kind),
        out_shape=jax.ShapeDtypeStruct((tokens, rows), jnp.bfloat16),
        grid=(pairs,),
        in_specs=[col, mat, vec, vec],
        out_specs=col,
        name="fast_output",
    )(queries, packed, gain.reshape(pairs, 1, 2 * size), bias.reshape(pairs, 1, 2 * size))


def fetch(fast):
    inner = lax.all_gather(fast.astype(jnp.bfloat16), "gy", axis=0, tiled=True)
    return lax.all_gather(inner, "gx", axis=0, tiled=True)


def collect(part):
    outer = lax.psum_scatter(part, "gx", scatter_dimension=0, tiled=True)
    return lax.psum_scatter(outer, "gy", scatter_dimension=0, tiled=True).astype(jnp.float32)


def per_device(
    key_rows, value_rows, query_rows, token_rates, fast_weights, momentum, norm_gain, norm_bias
):
    total = key_rows.shape[0] * lax.axis_size("gx") * lax.axis_size("gy")
    size = norm_gain.shape[1]
    rates = jnp.repeat(token_rates.astype(jnp.bfloat16), size, axis=1)
    fast, moment = (fast_weights, momentum)
    for step in range(STEPS):
        part = gradient(key_rows, value_rows, rates, fetch(fast), norm_gain, norm_bias, total, size, kind=KIND)
        grad = collect(part)
        moment = momentum_keep * moment + grad
        fast = fast - inner_rate * moment
    mixed = output(query_rows, fetch(fast), norm_gain, norm_bias, size, kind=KIND)
    return (mixed, fast, moment)


def solution(mesh):
    rows = P(("gx", "gy"), None)
    return jax.shard_map(
        per_device,
        mesh=mesh,
        in_specs=(rows,) * 6 + (P(), P()),
        out_specs=(rows,) * 3,
        check_vma=False,
    )
```

```python
import functools

import jax
import jax.numpy as jnp
from jax import lax
from jax.experimental import pallas as pl
from jax.experimental.pallas import tpu as pltpu
from jax.sharding import PartitionSpec as P

STEPS = 2

momentum_keep = 0.9
inner_rate = 0.5

GELU_SCALE = 0.7978845608028654
GELU_CUBIC = 0.044715
NT = (((1,), (1,)), ((), ()))
NN = (((1,), (0,)), ((), ()))
BF = jnp.bfloat16
F32 = jnp.float32


def dot(a, b, dims=NN):
    return lax.dot_general(a, b, dims, preferred_element_type=F32)


def blocks(packed, size):
    width = packed.shape[1] // 2
    top, low = packed[:size], packed[size:]

    def diagonal(a, b):
        a = jnp.concatenate([a, jnp.zeros_like(a)], axis=1)
        b = jnp.concatenate([jnp.zeros_like(b), b], axis=1)
        return jnp.concatenate([a, b], axis=0).astype(BF)

    def centred(a):
        a = a[:, width:].astype(F32)
        return a - jnp.mean(a, axis=0, keepdims=True)

    return diagonal(top[:, :width], low[:, :width]), diagonal(centred(top), centred(low))


def pair_mean(size):
    row = lax.broadcasted_iota(jnp.int32, (2 * size, 2 * size), 0) // size
    col = lax.broadcasted_iota(jnp.int32, (2 * size, 2 * size), 1) // size
    return jnp.where(row == col, 1.0 / size, 0.0).astype(BF)


def activate(first, kind, slope_too):
    const = lambda x: jnp.asarray(x, kind)
    first = first.astype(kind)
    square = first * first
    inner = first * (square * const(GELU_SCALE * GELU_CUBIC) + const(GELU_SCALE))
    half = jnp.tanh(inner) * const(0.5) + const(0.5)
    active = first * half
    if not slope_too:
        return active.astype(BF)
    poly = square * const(6 * GELU_SCALE * GELU_CUBIC) + const(2 * GELU_SCALE)
    slope = half + (active - active * half) * poly
    return active.astype(BF), slope.astype(BF)


def grad_kernel(cfg, place_ref, *refs):
    (size, chunk, skew, kind, total) = cfg
    key_own, value_own, rate_own, key_far, value_far, rate_far = refs[:6]
    members = (len(refs) - 14) // 2
    weight_refs = refs[6 : 6 + members]
    gain_ref, bias_ref = refs[6 + members : 8 + members]
    out_refs = refs[8 + members : 8 + 2 * members]
    whole_ref, sums_ref, active_ref, dfirst_ref, dsecond_ref, slope_ref = refs[-6:]
    step = pl.program_id(0)
    mine = place_ref[2]
    groups, rows_own, two = weight_refs[0].shape
    width = two // 2
    span = members * rows_own

    @pl.when(step == 0)
    def _():
        for rel, w in enumerate(weight_refs):
            at = pl.multiple_of((mine ^ rel) * rows_own, rows_own)
            for g in range(groups):
                whole_ref[pl.ds(g * span + at, rows_own), :] = w[g]

    base = pl.multiple_of(step * 2 * size, 2 * size)
    first_w, second_w = blocks(whole_ref[pl.ds(base, 2 * size), :], size)
    mean = pair_mean(size)
    gain = gain_ref[0]
    bias = bias_ref[0]
    scaled = gain * (1.0 / total)
    tokens = key_own.shape[0]
    pieces = [(src, at) for src in ((key_own, value_own, rate_own, 0), (key_far, value_far, rate_far, tokens)) for at in range(0, tokens, chunk)]
    state = {}

    def s0(i):
        (key, value, rate, off), at = pieces[i]
        state[i, "first"] = dot(key[pl.ds(at, chunk), :], first_w)

    def s1(i):
        (key, value, rate, off), at = pieces[i]
        rows = pl.ds(off + at, chunk)
        active, slope = activate(state.pop((i, "first")), kind, True)
        active_ref[rows, :] = active
        slope_ref[rows, :] = slope
        state[i, "centre"] = dot(active, second_w, NT)

    def s2(i):
        centre = state[i, "centre"]
        state[i, "spread"] = dot((centre * centre).astype(BF), mean)

    def s3(i):
        (key, value, rate, off), at = pieces[i]
        rows = pl.ds(at, chunk)
        inverse = lax.rsqrt(state.pop((i, "spread")) + 1e-06)
        unit = state.pop((i, "centre")) * inverse
        target = value[rows, :].astype(F32) - key[rows, :].astype(F32)
        error = unit * gain + (bias - target)
        dunit = error * (rate[rows, :].astype(F32) * scaled)
        state[i, "along"] = dot((dunit * unit).astype(BF), mean)
        state[i, "rest"] = (inverse, unit, dunit)

    def s4(i):
        (key, value, rate, off), at = pieces[i]
        inverse, unit, dunit = state.pop((i, "rest"))
        dsecond = (inverse * (dunit - unit * state.pop((i, "along")))).astype(BF)
        dsecond_ref[pl.ds(off + at, chunk), :] = dsecond
        state[i, "dactive"] = dot(dsecond, second_w)

    def s5(i):
        (key, value, rate, off), at = pieces[i]
        rows = pl.ds(off + at, chunk)
        dfirst_ref[rows, :] = state.pop((i, "dactive")).astype(BF) * slope_ref[rows, :]

    stages = (s0, s1, s2, s3, s4, s5)
    n = len(pieces)
    if skew is None:
        for i in range(n):
            for s in stages: s(i)
    else:
        for t in range(n + max(skew)):
            for s, lag in list(zip(stages, skew))[::-1]:
                if 0 <= t - lag < n:
                    s(t - lag)
    dsecond_t = dsecond_ref[...].T
    key_t = [key_own[...].T, key_far[...].T]
    for head in range(2):
        part = slice(head * size, (head + 1) * size)
        cols = slice(head * width, (head + 1) * width)
        first = dot(key_t[0][part], dfirst_ref[:tokens, cols]) + dot(key_t[1][part], dfirst_ref[tokens:, cols])
        second = dot(dsecond_t[part], active_ref[:, cols])
        second = second - jnp.mean(second, axis=0, keepdims=True)
        sums_ref[pl.ds(base + head * size, size), :width] = first.astype(BF)
        sums_ref[pl.ds(base + head * size, size), width:] = second.astype(BF)

    @pl.when(step == pl.num_programs(0) - 1)
    def _():
        for rel, o in enumerate(out_refs):
            at = pl.multiple_of((mine ^ rel) * rows_own, rows_own)
            for g in range(groups):
                o[g] = sums_ref[pl.ds(g * span + at, rows_own), :]


def gradient(place, own, far, weights, gain, bias, total, size, lag, chunk=128, skew=None, kind=BF, flags=None):
    tokens = own[0].shape[0]
    groups, rows_own, two = weights[0].shape
    members = len(weights)
    per = members * rows_own // (2 * size)
    zof = lambda i, place: place[0] ^ (i // per + lag)
    own_spec = pl.BlockSpec((tokens, 2 * size), lambda i, place: (0, (zof(i, place) * 2 + place[1]) * per + i % per))
    far_spec = pl.BlockSpec((tokens, 2 * size), lambda i, place: (0, zof(i, place) * per + i % per))
    vec = pl.BlockSpec((1, 1, 2 * size), lambda i, place: ((zof(i, place) * 2 + place[1]) * per + i % per, 0, 0))
    mat = pl.BlockSpec((groups, rows_own, two), lambda i, place: (0, 0, 0))
    out = jax.ShapeDtypeStruct((groups, rows_own, two), BF)
    cfg = (size, chunk, skew, kind, total)
    rows = groups * members * rows_own
    pairs = gain.size // (2 * size)
    return pl.pallas_call(
        functools.partial(grad_kernel, cfg),
        out_shape=[out] * members,
        grid_spec=pltpu.PrefetchScalarGridSpec(
            num_scalar_prefetch=1,
            grid=(groups * per,),
            in_specs=[own_spec] * 3 + [far_spec] * 2 + [own_spec] + [mat] * members + [vec, vec],
            out_specs=[mat] * members,
            scratch_shapes=[
                pltpu.VMEM((rows, two), BF),
                pltpu.VMEM((rows, two), BF),
                pltpu.VMEM((2 * tokens, two), BF),
                pltpu.VMEM((2 * tokens, two), BF),
                pltpu.VMEM((2 * tokens, 2 * size), BF),
                pltpu.VMEM((2 * tokens, two), BF),
            ],
        ),
        compiler_params=pltpu.CompilerParams(flags=flags) if flags else None,
        name="fast_gradient",
    )(place, *own, *far, *weights, gain.reshape(pairs, 1, 2 * size), bias.reshape(pairs, 1, 2 * size))


def output_kernel(size, chunk, kind, place_ref, query_ref, weight_ref, gain_ref, bias_ref, *refs):
    out_ref, whole_ref = refs[-2:]
    step = pl.program_id(0)
    mine = place_ref[2]
    members, groups, rows_own, _ = weight_ref.shape

    @pl.when(step == 0)
    def _():
        for rel in range(members):
            at = pl.multiple_of((mine ^ rel) * rows_own, rows_own)
            for g in range(groups):
                whole_ref[pl.ds(g * members * rows_own + at, rows_own), :] = weight_ref[rel, g]

    base = pl.multiple_of(step * 2 * size, 2 * size)
    first_w, second_w = blocks(whole_ref[pl.ds(base, 2 * size), :], size)
    mean = pair_mean(size)
    gain = gain_ref[0]
    bias = bias_ref[0]
    for at in range(0, query_ref.shape[0], chunk):
        rows = pl.ds(at, chunk)
        queries = query_ref[rows, :]
        active = activate(dot(queries, first_w), kind, False)
        centre = dot(active, second_w, NT)
        spread = dot((centre * centre).astype(BF), mean)
        unit = centre * lax.rsqrt(spread + 1e-06)
        out_ref[rows, :] = (queries.astype(F32) + unit * gain + bias).astype(BF)


def output(place, queries, weights, gain, bias, before, size, lag, flip, chunk=512, kind=BF):
    tokens, model = queries.shape
    members, groups, rows_own, two = weights.shape
    per = members * rows_own // (2 * size)
    pairs = gain.size // (2 * size)
    column = lambda i, place: ((place[0] ^ (i // per + lag)) * 2 + (place[1] ^ flip)) * per + i % per
    col = pl.BlockSpec((tokens, 2 * size), lambda i, place: (0, column(i, place)))
    vec = pl.BlockSpec((1, 1, 2 * size), lambda i, place: (column(i, place), 0, 0))
    mat = pl.BlockSpec((members, groups, rows_own, two), lambda i, place: (0, 0, 0, 0))
    more = [] if before is None else [before]
    return pl.pallas_call(
        functools.partial(output_kernel, size, chunk, kind),
        out_shape=jax.ShapeDtypeStruct((tokens, model), BF),
        grid_spec=pltpu.PrefetchScalarGridSpec(
            num_scalar_prefetch=1,
            grid=(groups * per,),
            in_specs=[col, mat, vec, vec] + [pl.BlockSpec(memory_space=pl.ANY)] * len(more),
            out_specs=col,
            scratch_shapes=[pltpu.VMEM((groups * members * rows_own, two), BF)],
        ),
        input_output_aliases={5: 0} if more else {},
        name="fast_output",
    )(place, queries, weights, gain.reshape(pairs, 1, 2 * size), bias.reshape(pairs, 1, 2 * size), *more)


def pick_kernel(place_ref, *refs):
    half = len(refs) // 2
    for source, target in zip(refs[:half], refs[half:]):
        target[...] = source[...]


def pick(place, arrays, groups, flip):
    tokens, model = arrays[0].shape
    wide = model // (2 * groups)
    return pl.pallas_call(
        pick_kernel,
        out_shape=[jax.ShapeDtypeStruct((tokens, groups * wide), a.dtype) for a in arrays],
        grid_spec=pltpu.PrefetchScalarGridSpec(
            num_scalar_prefetch=1,
            grid=(groups,),
            in_specs=[pl.BlockSpec((tokens, wide), lambda i, place: (0, 2 * i + (place[1] ^ flip)))] * len(arrays),
            out_specs=[pl.BlockSpec((tokens, wide), lambda i, place: (0, i))] * len(arrays),
        ),
        name="pick",
    )(place, *arrays)


def core_swap(x):
    n = lax.axis_size("gx")
    return lax.ppermute(x, "gx", [(i, i ^ 1) for i in range(n)])


def z_shift(x, s):
    n = lax.axis_size("gx")
    return lax.ppermute(x, "gx", [(i, i ^ (2 * s)) for i in range(n)])


def plane_shift(x, s):
    n = lax.axis_size("gy")
    return lax.ppermute(x, "gy", [(i, i ^ s) for i in range(n)])


def fetch(fast, groups, members, chunks):
    narrow = fast.astype(BF)
    held = [narrow] + [z_shift(narrow, s) for s in range(1, groups)]
    return [(lambda mine: [mine] + [plane_shift(mine, s) for s in range(1, members)])(jnp.stack(held[at : at + count])) for at, count in chunks]


def collect(parts, groups, members, chunks):
    sums = []
    for part, (at, count) in zip(parts, chunks):
        arrived = [plane_shift(part[s], s) for s in range(1, members)]
        for g in range(count):
            sums.append(sum([a[g].astype(F32) for a in [part[0]] + arrived]))
    total = sums[0]
    for s in range(1, groups):
        total = total + z_shift(sums[s].astype(BF), s).astype(F32)
    return total


def per_device(
    key_rows, value_rows, query_rows, token_rates, fast_weights, momentum, norm_gain, norm_bias
):
    size = norm_gain.shape[1]
    groups, members = lax.axis_size("gx") // 2, lax.axis_size("gy")
    total = key_rows.shape[0] * 2 * groups * members
    gx = lax.axis_index("gx")
    place = jnp.stack([gx // 2, gx % 2, lax.axis_index("gy")]).astype(jnp.int32)
    chunks = [(0, groups // 2), (groups // 2, groups - groups // 2)]
    fast, moment = (fast_weights, momentum)
    spread = lambda rates: jnp.repeat(rates.astype(BF), size, axis=1)
    weights = fetch(fast, groups, members, chunks)
    key_send, value_send = pick(place, (key_rows, value_rows), groups, 1)
    far = (core_swap(key_send), core_swap(value_send), spread(core_swap(token_rates)))
    own = (key_rows, value_rows, spread(token_rates))
    for step in range(STEPS):
        parts = [
            gradient(place, own, far, w, norm_gain, norm_bias, total, size, at, chunk=512)
            for w, (at, count) in zip(weights, chunks)
        ]
        grad = collect(parts, groups, members, chunks)
        moment = momentum_keep * moment + grad
        fast = fast - inner_rate * moment
        weights = fetch(fast, groups, members, chunks)
    mixed = None
    whole = [jnp.stack(w) for w in weights]
    twin = [core_swap(w) for w in whole]
    for flip, ws in enumerate((whole, twin)):
        for w, (at, count) in zip(ws, chunks):
            mixed = output(place, query_rows, w, norm_gain, norm_bias, mixed, size, at, flip)
    return (mixed, fast, moment)


def plain_grad_kernel(size, chunk, total, kind, key_ref, value_ref, rate_ref, packed_ref, gain_ref, bias_ref, out_ref,
                active_ref, dfirst_ref, dsecond_ref):
    tokens = key_ref.shape[0]
    width = packed_ref.shape[1] // 2
    first_w, second_w = blocks(packed_ref[...], size)
    mean = pair_mean(size)
    gain = gain_ref[0]
    bias = bias_ref[0]
    scaled = gain * (1.0 / total)
    for at in range(0, tokens, chunk):
        rows = pl.ds(at, chunk)
        keys = key_ref[rows, :]
        first = dot(keys, first_w)
        active, slope = activate(first, kind, True)
        active_ref[rows, :] = active
        centre = dot(active, second_w, NT)
        spread = dot((centre * centre).astype(jnp.bfloat16), mean)
        inverse = lax.rsqrt(spread + 1e-06)
        unit = centre * inverse
        target = value_ref[rows, :].astype(jnp.float32) - keys.astype(jnp.float32)
        error = unit * gain + (bias - target)
        dunit = error * (rate_ref[rows, :].astype(jnp.float32) * scaled)
        along = dot((dunit * unit).astype(jnp.bfloat16), mean)
        dsecond = (inverse * (dunit - unit * along)).astype(jnp.bfloat16)
        dsecond_ref[rows, :] = dsecond
        dactive = dot(dsecond, second_w)
        dfirst_ref[rows, :] = (dactive * slope.astype(F32)).astype(jnp.bfloat16)
    keys_t = key_ref[...].T
    dsecond_t = dsecond_ref[...].T
    for head in range(2):
        mine = slice(head * size, (head + 1) * size)
        cols = slice(head * width, (head + 1) * width)
        out_ref[mine, :width] = dot(keys_t[mine], dfirst_ref[:, cols]).astype(out_ref.dtype)
        second = dot(dsecond_t[mine], active_ref[:, cols])
        out_ref[mine, width:] = (second - jnp.mean(second, axis=0, keepdims=True)).astype(out_ref.dtype)

def plain_apply_kernel(size, chunk, kind, query_ref, packed_ref, gain_ref, bias_ref, out_ref):
    tokens = query_ref.shape[0]
    first_w, second_w = blocks(packed_ref[...], size)
    mean = pair_mean(size)
    gain = gain_ref[0]
    bias = bias_ref[0]
    for at in range(0, tokens, chunk):
        rows = pl.ds(at, chunk)
        queries = query_ref[rows, :]
        first = dot(queries, first_w)
        active = activate(first, kind, False)
        centre = dot(active, second_w, NT)
        spread = dot((centre * centre).astype(jnp.bfloat16), mean)
        unit = centre * lax.rsqrt(spread + 1e-06)
        out_ref[rows, :] = (queries.astype(jnp.float32) + unit * gain + bias).astype(out_ref.dtype)

def plain_gradient(keys, values, rates, packed, gain, bias, total, size, chunk=128, kind=jnp.float32):
    tokens = keys.shape[0]
    rows, two = packed.shape
    pairs = rows // (2 * size)
    col = pl.BlockSpec((tokens, 2 * size), lambda i: (0, i))
    vec = pl.BlockSpec((1, 1, 2 * size), lambda i: (i, 0, 0))
    mat = pl.BlockSpec((2 * size, two), lambda i: (i, 0))
    return pl.pallas_call(
        functools.partial(plain_grad_kernel, size, chunk, total, kind),
        out_shape=jax.ShapeDtypeStruct((rows, two), jnp.bfloat16),
        grid=(pairs,),
        in_specs=[col, col, col, mat, vec, vec],
        out_specs=mat,
        scratch_shapes=[pltpu.VMEM((tokens, two), jnp.bfloat16), pltpu.VMEM((tokens, two), jnp.bfloat16), pltpu.VMEM((tokens, 2 * size), jnp.bfloat16)],
        name="plain_gradient",
    )(keys, values, rates, packed, gain.reshape(pairs, 1, 2 * size), bias.reshape(pairs, 1, 2 * size))

def plain_output(queries, packed, gain, bias, size, chunk=128, kind=jnp.float32):
    tokens = queries.shape[0]
    rows, two = packed.shape
    pairs = rows // (2 * size)
    col = pl.BlockSpec((tokens, 2 * size), lambda i: (0, i))
    vec = pl.BlockSpec((1, 1, 2 * size), lambda i: (i, 0, 0))
    mat = pl.BlockSpec((2 * size, two), lambda i: (i, 0))
    return pl.pallas_call(
        functools.partial(plain_apply_kernel, size, chunk, kind),
        out_shape=jax.ShapeDtypeStruct((tokens, rows), jnp.bfloat16),
        grid=(pairs,),
        in_specs=[col, mat, vec, vec],
        out_specs=col,
        name="plain_output",
    )(queries, packed, gain.reshape(pairs, 1, 2 * size), bias.reshape(pairs, 1, 2 * size))


def plain_device(
    key_rows, value_rows, query_rows, token_rates, fast_weights, momentum, norm_gain, norm_bias
):
    size = norm_gain.shape[1]
    total = key_rows.shape[0] * lax.axis_size("gx") * lax.axis_size("gy")
    place = jnp.zeros((3,), jnp.int32)
    rates = jnp.repeat(token_rates.astype(BF), size, axis=1)
    fast, moment = (fast_weights, momentum)

    def whole(fast):
        inner = lax.all_gather(fast.astype(BF), "gy", axis=0, tiled=True)
        return lax.all_gather(inner, "gx", axis=0, tiled=True)

    for step in range(STEPS):
        part = plain_gradient(key_rows, value_rows, rates, whole(fast), norm_gain, norm_bias, total, size)
        outer = lax.psum_scatter(part, "gx", scatter_dimension=0, tiled=True)
        grad = lax.psum_scatter(outer, "gy", scatter_dimension=0, tiled=True).astype(F32)
        moment = momentum_keep * moment + grad
        fast = fast - inner_rate * moment
    mixed = plain_output(query_rows, whole(fast), norm_gain, norm_bias, size)
    return (mixed, fast, moment)


def power_of_two(n):
    return n > 0 and n & (n - 1) == 0


def solution(mesh):
    rows = P(("gx", "gy"), None)

    def run(*args):
        rows_own = args[0].shape[1] // mesh.size
        size = args[6].shape[1]
        gx, gy = mesh.shape["gx"], mesh.shape["gy"]
        paired = gx % 4 == 0 and power_of_two(gx) and power_of_two(gy)
        even = rows_own % 32 == 0 and (rows_own * gy) % (2 * size) == 0
        body = per_device if paired and even else plain_device
        return jax.shard_map(
            body,
            mesh=mesh,
            in_specs=(rows,) * 6 + (P(), P()),
            out_specs=(rows,) * 3,
            check_vma=False,
        )(*args)

    return run
```

```python
import functools

import jax
import jax.numpy as jnp
from jax import lax
from jax.experimental import pallas as pl
from jax.experimental.pallas import tpu as pltpu
from jax.sharding import PartitionSpec as P

STEPS = 2

momentum_keep = 0.9
inner_rate = 0.5

GELU_SCALE = 0.7978845608028654
GELU_CUBIC = 0.044715
NT = (((1,), (1,)), ((), ()))
NN = (((1,), (0,)), ((), ()))
BF = jnp.bfloat16
F32 = jnp.float32


def dot(a, b, dims=NN):
    return lax.dot_general(a, b, dims, preferred_element_type=F32)


def blocks(packed, size):
    width = packed.shape[1] // 2
    top, low = packed[:size], packed[size:]

    def diagonal(a, b):
        a = jnp.concatenate([a, jnp.zeros_like(a)], axis=1)
        b = jnp.concatenate([jnp.zeros_like(b), b], axis=1)
        return jnp.concatenate([a, b], axis=0).astype(BF)

    def centred(a):
        a = a[:, width:].astype(F32)
        return a - jnp.mean(a, axis=0, keepdims=True)

    return diagonal(top[:, :width], low[:, :width]), diagonal(centred(top), centred(low))


def head_mean(size, heads):
    row = lax.broadcasted_iota(jnp.int32, (heads * size, heads * size), 0) // size
    col = lax.broadcasted_iota(jnp.int32, (heads * size, heads * size), 1) // size
    return jnp.where(row == col, 1.0 / size, 0.0).astype(BF)


def averaged(x, mean):
    half, wide = x.shape[0] // 2, x.shape[1]
    both = dot(jnp.concatenate([x[:half], x[half:]], axis=1), mean)
    return jnp.concatenate([both[:, :wide], both[:, wide:]], axis=0)


def pair_row(ref, pair):
    return jnp.concatenate([ref[pl.ds(2 * pair, 1), :], ref[pl.ds(2 * pair + 1, 1), :]], axis=1)


def fill(whole_ref, parts, mine, rows_own):
    for rel, part in enumerate(parts):
        at = pl.multiple_of((mine ^ rel) * rows_own, rows_own)
        for g in range(part.shape[0]):
            whole_ref[pl.ds(g * len(parts) * rows_own + at, rows_own), :] = part[g]


def staggered(stages, lags, n):
    for t in range(n + max(lags)):
        for stage, lag in sorted(zip(stages, lags), key=lambda item: -item[1]):
            if 0 <= t - lag < n:
                stage(t - lag)


def activate(first, kind, slope_too):
    const = lambda x: jnp.asarray(x, kind)
    first = first.astype(kind)
    square = first * first
    inner = first * (square * const(GELU_SCALE * GELU_CUBIC) + const(GELU_SCALE))
    half = jnp.tanh(inner) * const(0.5) + const(0.5)
    active = first * half
    if not slope_too:
        return active.astype(BF)
    poly = square * const(6 * GELU_SCALE * GELU_CUBIC) + const(2 * GELU_SCALE)
    slope = half + (active - active * half) * poly
    return active.astype(BF), slope.astype(BF)


def grad_kernel(size, lags, pairs, per, lag, total, place_ref, *refs):
    key_own, value_own, key_far, value_far, rate_own, rate_far = refs[:6]
    members = (len(refs) - 15) // 2
    weight_refs = refs[6 : 6 + members]
    gain_ref, bias_ref = refs[6 + members : 8 + members]
    out_refs = refs[8 + members : 8 + 2 * members]
    whole_ref, sums_ref, active_ref, dfirst_ref, dsecond_ref, slope_ref, rate_ref = refs[-7:]
    step = pl.program_id(0)
    mine = place_ref[2]
    groups, rows_own, two = weight_refs[0].shape
    width = two // 2
    tokens = key_own.shape[0]
    heads = rate_own.shape[0]

    @pl.when(step == 0)
    def _():
        fill(whole_ref, weight_refs, mine, rows_own)
        rate_ref[:tokens, :] = rate_own[...].T.astype(BF)
        rate_ref[tokens:, :] = rate_far[...].T.astype(BF)

    mean = head_mean(size, 4)
    head_row = lax.broadcasted_iota(jnp.int32, (heads, 2 * size), 0)
    head_col = lax.broadcasted_iota(jnp.int32, (heads, 2 * size), 1) // size
    zof = place_ref[0] ^ (step * pairs // per + lag)
    first_pair = (zof * 2 + place_ref[1]) * per + (step * pairs) % per
    const, state = [], {}
    for j in range(pairs):
        base = pl.multiple_of((step * pairs + j) * 2 * size, 2 * size)
        gain = pair_row(gain_ref, first_pair + j)
        pick = jnp.where(head_row == 2 * (first_pair + j) + head_col, 1.0, 0.0).astype(BF)
        const.append((base, blocks(whole_ref[pl.ds(base, 2 * size), :], size), gain, pair_row(bias_ref, first_pair + j), gain * (1.0 / total), pick))
    sources = ((key_own, value_own), (key_far, value_far))

    def at(i):
        j, far = divmod(i, 2)
        return j, sources[far], slice(2 * size * j, 2 * size * (j + 1)), pl.ds(far * tokens, tokens), pl.ds(i * tokens, tokens)

    def enter(i):
        j, (key, value), cols, rows, own = at(i)
        state[i, "first"] = dot(key[:, cols], const[j][1][0]).astype(BF)

    def bend(i):
        j, (key, value), cols, rows, own = at(i)
        active, slope = activate(state.pop((i, "first")), BF, True)
        active_ref[own, :] = active
        slope_ref[own, :] = slope
        state[i, "centre"] = dot(active, const[j][1][1], NT)

    def measure(i):
        centre = state[i, "centre"]
        state[i, "spread"] = averaged((centre * centre).astype(BF), mean)
        state[i, "rate"] = dot(rate_ref[at(i)[3], :], const[at(i)[0]][5])

    def compare(i):
        j, (key, value), cols, rows, own = at(i)
        base, mats, gain, bias, scaled, pick = const[j]
        inverse = lax.rsqrt(state.pop((i, "spread")) + 1e-06)
        unit = state.pop((i, "centre")) * inverse
        target = value[:, cols].astype(F32) - key[:, cols].astype(F32)
        error = unit * gain + (bias - target)
        dunit = error * (state.pop((i, "rate")) * scaled)
        state[i, "along"] = averaged((dunit * unit).astype(BF), mean)
        state[i, "rest"] = (inverse, unit, dunit)

    def back(i):
        j, (key, value), cols, rows, own = at(i)
        inverse, unit, dunit = state.pop((i, "rest"))
        dsecond = (inverse * (dunit - unit * state.pop((i, "along")))).astype(BF)
        dsecond_ref[own, :] = dsecond
        state[i, "dactive"] = dot(dsecond, const[j][1][1]).astype(BF)

    def leave(i):
        j, (key, value), cols, rows, own = at(i)
        dfirst_ref[own, :] = state.pop((i, "dactive")) * slope_ref[own, :]

    def gather(i):
        j, (key, value), cols, rows, own = at(i)
        if i % 2 == 0:
            return
        base = const[j][0]
        both = pl.ds((i - 1) * tokens, 2 * tokens)
        key_t = [source[0][:, cols].T for source in sources]
        dsecond_t = dsecond_ref[both, :].T
        for head in range(2):
            part = slice(head * size, (head + 1) * size)
            lane = slice(head * width, (head + 1) * width)
            halves = [dfirst_ref[pl.ds(k * tokens, tokens), lane] for k in (i - 1, i)]
            first = dot(key_t[0][part], halves[0]) + dot(key_t[1][part], halves[1])
            second = dot(dsecond_t[part], active_ref[both, lane])
            second = second - jnp.mean(second, axis=0, keepdims=True)
            sums_ref[pl.ds(base + head * size, size), :width] = first.astype(BF)
            sums_ref[pl.ds(base + head * size, size), width:] = second.astype(BF)

    staggered((enter, bend, measure, compare, back, leave, gather), lags, 2 * pairs)

    @pl.when(step == pl.num_programs(0) - 1)
    def _():
        for rel, out in enumerate(out_refs):
            at = pl.multiple_of((mine ^ rel) * rows_own, rows_own)
            for g in range(groups):
                out[g] = sums_ref[pl.ds(g * members * rows_own + at, rows_own), :]


def gradient(place, own, far, rates, weights, gain, bias, total, lag, pairs=1, lags=(0, 1, 2, 3, 4, 5, 6)):
    tokens = own[0].shape[0]
    heads, size = gain.shape
    members = len(weights)
    groups, rows_own, two = weights[0].shape
    per = members * rows_own // (2 * size)
    zof = lambda i, place: place[0] ^ (i * pairs // per + lag)
    wide = pairs * 2 * size
    own_spec = pl.BlockSpec((tokens, wide), lambda i, place: (0, ((zof(i, place) * 2 + place[1]) * per + i * pairs % per) // pairs))
    far_spec = pl.BlockSpec((tokens, wide), lambda i, place: (0, (zof(i, place) * per + i * pairs % per) // pairs))
    whole = lambda shape: pl.BlockSpec(shape, lambda i, place: (0,) * len(shape))
    mat = whole((groups, rows_own, two))
    rows = groups * members * rows_own
    return pl.pallas_call(
        functools.partial(grad_kernel, size, lags, pairs, per, lag, total),
        out_shape=[jax.ShapeDtypeStruct((groups, rows_own, two), BF)] * members,
        grid_spec=pltpu.PrefetchScalarGridSpec(
            num_scalar_prefetch=1,
            grid=(groups * per // pairs,),
            in_specs=[own_spec] * 2 + [far_spec] * 2 + [whole((heads, tokens))] * 2 + [mat] * members + [whole((heads, size))] * 2,
            out_specs=[mat] * members,
            scratch_shapes=[
                pltpu.VMEM((rows, two), BF),
                pltpu.VMEM((rows, two), BF),
                pltpu.VMEM((2 * pairs * tokens, two), BF),
                pltpu.VMEM((2 * pairs * tokens, two), BF),
                pltpu.VMEM((2 * pairs * tokens, 2 * size), BF),
                pltpu.VMEM((2 * pairs * tokens, two), BF),
                pltpu.VMEM((2 * tokens, heads), BF),
            ],
        ),
        name="fast_gradient",
    )(place, *own, *far, *rates, *weights, gain, bias)


def output_kernel(size, chunk, lags, pairs, per, lag, flip, place_ref, query_ref, weight_ref, gain_ref, bias_ref, *refs):
    out_ref, whole_ref = refs[-2:]
    step = pl.program_id(0)
    members, groups, rows_own, two = weight_ref.shape

    @pl.when(step == 0)
    def _():
        fill(whole_ref, [weight_ref.at[rel] for rel in range(members)], place_ref[2], rows_own)

    mean = head_mean(size, 4)
    zof = place_ref[0] ^ (step * pairs // per + lag)
    first_pair = (zof * 2 + (place_ref[1] ^ flip)) * per + (step * pairs) % per
    const, state = [], {}
    for j in range(pairs):
        base = pl.multiple_of((step * pairs + j) * 2 * size, 2 * size)
        const.append((blocks(whole_ref[pl.ds(base, 2 * size), :], size), pair_row(gain_ref, first_pair + j), pair_row(bias_ref, first_pair + j)))
    count = query_ref.shape[0] // chunk

    def at(i):
        j, k = divmod(i, count)
        return const[j], (pl.ds(k * chunk, chunk), slice(2 * size * j, 2 * size * (j + 1)))

    def enter(i):
        (mats, gain, bias), where = at(i)
        state[i, "first"] = dot(query_ref[where], mats[0]).astype(BF)

    def bend(i):
        (mats, gain, bias), where = at(i)
        state[i, "centre"] = dot(activate(state.pop((i, "first")), BF, False), mats[1], NT)

    def measure(i):
        centre = state[i, "centre"]
        state[i, "spread"] = averaged((centre * centre).astype(BF), mean)

    def leave(i):
        (mats, gain, bias), where = at(i)
        unit = state.pop((i, "centre")) * lax.rsqrt(state.pop((i, "spread")) + 1e-06)
        out_ref[where] = (query_ref[where].astype(F32) + unit * gain + bias).astype(BF)

    staggered((enter, bend, measure, leave), lags, pairs * count)


def output(place, queries, weights, gain, bias, before, lag, flip, pairs=1, chunk=256, lags=(0, 1, 2, 3)):
    tokens, model = queries.shape
    members, groups, rows_own, two = weights.shape
    heads, size = gain.shape
    per = members * rows_own // (2 * size)
    column = lambda i, place: (((place[0] ^ (i * pairs // per + lag)) * 2 + (place[1] ^ flip)) * per + i * pairs % per) // pairs
    col = pl.BlockSpec((tokens, pairs * 2 * size), lambda i, place: (0, column(i, place)))
    whole = lambda shape: pl.BlockSpec(shape, lambda i, place: (0,) * len(shape))
    more = [] if before is None else [before]
    return pl.pallas_call(
        functools.partial(output_kernel, size, chunk, lags, pairs, per, lag, flip),
        out_shape=jax.ShapeDtypeStruct((tokens, model), BF),
        grid_spec=pltpu.PrefetchScalarGridSpec(
            num_scalar_prefetch=1,
            grid=(groups * per // pairs,),
            in_specs=[col, whole(weights.shape)] + [whole((heads, size))] * 2 + [pl.BlockSpec(memory_space=pl.ANY)] * len(more),
            out_specs=col,
            scratch_shapes=[pltpu.VMEM((groups * members * rows_own, two), BF)],
        ),
        input_output_aliases={5: 0} if more else {},
        name="fast_output",
    )(place, queries, weights, gain, bias, *more)


def pick_kernel(place_ref, *refs):
    half = len(refs) // 2
    for source, target in zip(refs[:half], refs[half:]):
        target[...] = source[...]


def pick(place, arrays, groups, flip):
    tokens, model = arrays[0].shape
    wide = model // (2 * groups)
    return pl.pallas_call(
        pick_kernel,
        out_shape=[jax.ShapeDtypeStruct((tokens, groups * wide), a.dtype) for a in arrays],
        grid_spec=pltpu.PrefetchScalarGridSpec(
            num_scalar_prefetch=1,
            grid=(groups,),
            in_specs=[pl.BlockSpec((tokens, wide), lambda i, place: (0, 2 * i + (place[1] ^ flip)))] * len(arrays),
            out_specs=[pl.BlockSpec((tokens, wide), lambda i, place: (0, i))] * len(arrays),
        ),
        name="pick",
    )(place, *arrays)


def core_swap(x):
    n = lax.axis_size("gx")
    return lax.ppermute(x, "gx", [(i, i ^ 1) for i in range(n)])


def z_shift(x, s):
    n = lax.axis_size("gx")
    return lax.ppermute(x, "gx", [(i, i ^ (2 * s)) for i in range(n)])


def plane_shift(x, s):
    n = lax.axis_size("gy")
    return lax.ppermute(x, "gy", [(i, i ^ s) for i in range(n)])


def fetch(fast, groups, members, chunks):
    narrow = fast.astype(BF)
    held = [narrow] + [z_shift(narrow, s) for s in range(1, groups)]
    return [(lambda mine: [mine] + [plane_shift(mine, s) for s in range(1, members)])(jnp.stack(held[at : at + count])) for at, count in chunks]


def collect(parts, groups, members, chunks):
    sums = []
    for part, (at, count) in zip(parts, chunks):
        arrived = [plane_shift(part[s], s) for s in range(1, members)]
        for g in range(count):
            sums.append(sum([a[g].astype(F32) for a in [part[0]] + arrived]))
    total = sums[0]
    for s in range(1, groups):
        total = total + z_shift(sums[s].astype(BF), s).astype(F32)
    return total


def per_device(
    key_rows, value_rows, query_rows, token_rates, fast_weights, momentum, norm_gain, norm_bias
):
    size = norm_gain.shape[1]
    groups, members = lax.axis_size("gx") // 2, lax.axis_size("gy")
    total = key_rows.shape[0] * 2 * groups * members
    gx = lax.axis_index("gx")
    place = jnp.stack([gx // 2, gx % 2, lax.axis_index("gy")]).astype(jnp.int32)
    chunks = [(0, groups // 2), (groups // 2, groups - groups // 2)]
    fast, moment = (fast_weights, momentum)
    weights = fetch(fast, groups, members, chunks)
    key_send, value_send = pick(place, (key_rows, value_rows), groups, 1)
    far = (core_swap(key_send), core_swap(value_send))
    own = (key_rows, value_rows)
    rates = (token_rates.T, core_swap(token_rates).T)
    pairs = members * fast.shape[0] // (2 * size)
    pairs = pairs if pairs <= 3 else 1
    for step in range(STEPS):
        parts = [
            gradient(place, own, far, rates, w, norm_gain, norm_bias, total, at, pairs)
            for w, (at, count) in zip(weights, chunks)
        ]
        grad = collect(parts, groups, members, chunks)
        moment = momentum_keep * moment + grad
        fast = fast - inner_rate * moment
        weights = fetch(fast, groups, members, chunks)
    mixed = None
    whole = [jnp.stack(w) for w in weights]
    twin = [core_swap(w) for w in whole]
    for flip, ws in enumerate((whole, twin)):
        for w, (at, count) in zip(ws, chunks):
            mixed = output(place, query_rows, w, norm_gain, norm_bias, mixed, at, flip, pairs, min(512, query_rows.shape[0]))
    return (mixed, fast, moment)


def plain_grad_kernel(size, chunk, total, kind, key_ref, value_ref, rate_ref, packed_ref, gain_ref, bias_ref, out_ref,
                active_ref, dfirst_ref, dsecond_ref):
    tokens = key_ref.shape[0]
    width = packed_ref.shape[1] // 2
    first_w, second_w = blocks(packed_ref[...], size)
    mean = head_mean(size, 2)
    gain = gain_ref[0]
    bias = bias_ref[0]
    scaled = gain * (1.0 / total)
    for at in range(0, tokens, chunk):
        rows = pl.ds(at, chunk)
        keys = key_ref[rows, :]
        first = dot(keys, first_w)
        active, slope = activate(first, kind, True)
        active_ref[rows, :] = active
        centre = dot(active, second_w, NT)
        spread = dot((centre * centre).astype(jnp.bfloat16), mean)
        inverse = lax.rsqrt(spread + 1e-06)
        unit = centre * inverse
        target = value_ref[rows, :].astype(jnp.float32) - keys.astype(jnp.float32)
        error = unit * gain + (bias - target)
        dunit = error * (rate_ref[rows, :].astype(jnp.float32) * scaled)
        along = dot((dunit * unit).astype(jnp.bfloat16), mean)
        dsecond = (inverse * (dunit - unit * along)).astype(jnp.bfloat16)
        dsecond_ref[rows, :] = dsecond
        dactive = dot(dsecond, second_w)
        dfirst_ref[rows, :] = (dactive * slope.astype(F32)).astype(jnp.bfloat16)
    keys_t = key_ref[...].T
    dsecond_t = dsecond_ref[...].T
    for head in range(2):
        mine = slice(head * size, (head + 1) * size)
        cols = slice(head * width, (head + 1) * width)
        out_ref[mine, :width] = dot(keys_t[mine], dfirst_ref[:, cols]).astype(out_ref.dtype)
        second = dot(dsecond_t[mine], active_ref[:, cols])
        out_ref[mine, width:] = (second - jnp.mean(second, axis=0, keepdims=True)).astype(out_ref.dtype)

def plain_apply_kernel(size, chunk, kind, query_ref, packed_ref, gain_ref, bias_ref, out_ref):
    tokens = query_ref.shape[0]
    first_w, second_w = blocks(packed_ref[...], size)
    mean = head_mean(size, 2)
    gain = gain_ref[0]
    bias = bias_ref[0]
    for at in range(0, tokens, chunk):
        rows = pl.ds(at, chunk)
        queries = query_ref[rows, :]
        first = dot(queries, first_w)
        active = activate(first, kind, False)
        centre = dot(active, second_w, NT)
        spread = dot((centre * centre).astype(jnp.bfloat16), mean)
        unit = centre * lax.rsqrt(spread + 1e-06)
        out_ref[rows, :] = (queries.astype(jnp.float32) + unit * gain + bias).astype(out_ref.dtype)

def plain_gradient(keys, values, rates, packed, gain, bias, total, size, chunk=128, kind=jnp.float32):
    tokens = keys.shape[0]
    rows, two = packed.shape
    pairs = rows // (2 * size)
    col = pl.BlockSpec((tokens, 2 * size), lambda i: (0, i))
    vec = pl.BlockSpec((1, 1, 2 * size), lambda i: (i, 0, 0))
    mat = pl.BlockSpec((2 * size, two), lambda i: (i, 0))
    return pl.pallas_call(
        functools.partial(plain_grad_kernel, size, chunk, total, kind),
        out_shape=jax.ShapeDtypeStruct((rows, two), jnp.bfloat16),
        grid=(pairs,),
        in_specs=[col, col, col, mat, vec, vec],
        out_specs=mat,
        scratch_shapes=[pltpu.VMEM((tokens, two), jnp.bfloat16), pltpu.VMEM((tokens, two), jnp.bfloat16), pltpu.VMEM((tokens, 2 * size), jnp.bfloat16)],
        name="plain_gradient",
    )(keys, values, rates, packed, gain.reshape(pairs, 1, 2 * size), bias.reshape(pairs, 1, 2 * size))

def plain_output(queries, packed, gain, bias, size, chunk=128, kind=jnp.float32):
    tokens = queries.shape[0]
    rows, two = packed.shape
    pairs = rows // (2 * size)
    col = pl.BlockSpec((tokens, 2 * size), lambda i: (0, i))
    vec = pl.BlockSpec((1, 1, 2 * size), lambda i: (i, 0, 0))
    mat = pl.BlockSpec((2 * size, two), lambda i: (i, 0))
    return pl.pallas_call(
        functools.partial(plain_apply_kernel, size, chunk, kind),
        out_shape=jax.ShapeDtypeStruct((tokens, rows), jnp.bfloat16),
        grid=(pairs,),
        in_specs=[col, mat, vec, vec],
        out_specs=col,
        name="plain_output",
    )(queries, packed, gain.reshape(pairs, 1, 2 * size), bias.reshape(pairs, 1, 2 * size))


def plain_device(
    key_rows, value_rows, query_rows, token_rates, fast_weights, momentum, norm_gain, norm_bias
):
    size = norm_gain.shape[1]
    total = key_rows.shape[0] * lax.axis_size("gx") * lax.axis_size("gy")
    place = jnp.zeros((3,), jnp.int32)
    rates = jnp.repeat(token_rates.astype(BF), size, axis=1)
    fast, moment = (fast_weights, momentum)

    def whole(fast):
        inner = lax.all_gather(fast.astype(BF), "gy", axis=0, tiled=True)
        return lax.all_gather(inner, "gx", axis=0, tiled=True)

    for step in range(STEPS):
        part = plain_gradient(key_rows, value_rows, rates, whole(fast), norm_gain, norm_bias, total, size)
        outer = lax.psum_scatter(part, "gx", scatter_dimension=0, tiled=True)
        grad = lax.psum_scatter(outer, "gy", scatter_dimension=0, tiled=True).astype(F32)
        moment = momentum_keep * moment + grad
        fast = fast - inner_rate * moment
    mixed = plain_output(query_rows, whole(fast), norm_gain, norm_bias, size)
    return (mixed, fast, moment)


def power_of_two(n):
    return n > 0 and n & (n - 1) == 0


def solution(mesh):
    rows = P(("gx", "gy"), None)

    def run(*args):
        rows_own = args[0].shape[1] // mesh.size
        size = args[6].shape[1]
        gx, gy = mesh.shape["gx"], mesh.shape["gy"]
        paired = gx % 4 == 0 and power_of_two(gx) and power_of_two(gy)
        even = rows_own % 32 == 0 and (rows_own * gy) % (2 * size) == 0
        body = per_device if paired and even else plain_device
        return jax.shard_map(
            body,
            mesh=mesh,
            in_specs=(rows,) * 6 + (P(), P()),
            out_specs=(rows,) * 3,
            check_vma=False,
        )(*args)

    return run
```

```python
import functools

import jax
import jax.numpy as jnp
from jax import lax
from jax.experimental import pallas as pl
from jax.experimental.pallas import tpu as pltpu
from jax.sharding import PartitionSpec as P


STEPS = 2

momentum_keep = 0.9
inner_rate = 0.5

GELU_SCALE = 0.7978845608028654
GELU_CUBIC = 0.044715
NT = (((1,), (1,)), ((), ()))
NN = (((1,), (0,)), ((), ()))
BF = jnp.bfloat16
F32 = jnp.float32


def dot(a, b, dims=NN):
    return lax.dot_general(a, b, dims, preferred_element_type=F32)


def blocks(packed, size):
    width = packed.shape[1] // 2
    top, low = packed[:size], packed[size:]

    def diagonal(a, b):
        a = jnp.concatenate([a, jnp.zeros_like(a)], axis=1)
        b = jnp.concatenate([jnp.zeros_like(b), b], axis=1)
        return jnp.concatenate([a, b], axis=0).astype(BF)

    def centred(a):
        a = a[:, width:].astype(F32)
        return a - jnp.mean(a, axis=0, keepdims=True)

    return diagonal(top[:, :width], low[:, :width]), diagonal(centred(top), centred(low))


def head_mean(size, heads):
    row = lax.broadcasted_iota(jnp.int32, (heads * size, heads * size), 0) // size
    col = lax.broadcasted_iota(jnp.int32, (heads * size, heads * size), 1) // size
    return jnp.where(row == col, 1.0 / size, 0.0).astype(BF)


def averaged(x, mean):
    half, wide = x.shape[0] // 2, x.shape[1]
    both = dot(jnp.concatenate([x[:half], x[half:]], axis=1), mean)
    return jnp.concatenate([both[:, :wide], both[:, wide:]], axis=0)


def pair_row(ref, pair):
    return jnp.concatenate([ref[pl.ds(2 * pair, 1), :], ref[pl.ds(2 * pair + 1, 1), :]], axis=1)


def fill(whole_ref, parts, mine, rows_own):
    for rel, part in enumerate(parts):
        at = pl.multiple_of((mine ^ rel) * rows_own, rows_own)
        for g in range(part.shape[0]):
            whole_ref[pl.ds(g * len(parts) * rows_own + at, rows_own), :] = part[g]


def staggered(stages, lags, n):
    for t in range(n + max(lags)):
        for stage, lag in sorted(zip(stages, lags), key=lambda item: -item[1]):
            if 0 <= t - lag < n:
                stage(t - lag)


def activate(first, kind, slope_too):
    const = lambda x: jnp.asarray(x, kind)
    first = first.astype(kind)
    square = first * first
    inner = first * (square * const(GELU_SCALE * GELU_CUBIC) + const(GELU_SCALE))
    half = jnp.tanh(inner) * const(0.5) + const(0.5)
    active = first * half
    if not slope_too:
        return active.astype(BF)
    poly = square * const(6 * GELU_SCALE * GELU_CUBIC) + const(2 * GELU_SCALE)
    slope = half + (active - active * half) * poly
    return active.astype(BF), slope.astype(BF)


def grad_kernel(size, lags, pairs, per, lag, total, place_ref, *refs):
    key_own, value_own, key_far, value_far, rate_own, rate_far = refs[:6]
    members = (len(refs) - 15) // 2
    weight_refs = refs[6 : 6 + members]
    gain_ref, bias_ref = refs[6 + members : 8 + members]
    out_refs = refs[8 + members : 8 + 2 * members]
    whole_ref, sums_ref, active_ref, dfirst_ref, dsecond_ref, slope_ref, rate_ref = refs[-7:]
    step = pl.program_id(0)
    mine = place_ref[2]
    groups, rows_own, two = weight_refs[0].shape
    width = two // 2
    tokens = key_own.shape[0]
    heads = rate_own.shape[0]

    @pl.when(step == 0)
    def _():
        fill(whole_ref, weight_refs, mine, rows_own)
        rate_ref[:tokens, :] = rate_own[...].T.astype(BF)
        rate_ref[tokens:, :] = rate_far[...].T.astype(BF)

    mean = head_mean(size, 4)
    head_row = lax.broadcasted_iota(jnp.int32, (heads, 2 * size), 0)
    head_col = lax.broadcasted_iota(jnp.int32, (heads, 2 * size), 1) // size
    zof = place_ref[0] ^ (step * pairs // per + lag)
    first_pair = (zof * 2 + place_ref[1]) * per + (step * pairs) % per
    const, state = [], {}
    for j in range(pairs):
        base = pl.multiple_of((step * pairs + j) * 2 * size, 2 * size)
        gain = pair_row(gain_ref, first_pair + j)
        pick = jnp.where(head_row == 2 * (first_pair + j) + head_col, 1.0, 0.0).astype(BF)
        const.append((base, blocks(whole_ref[pl.ds(base, 2 * size), :], size), gain, pair_row(bias_ref, first_pair + j), gain * (1.0 / total), pick))
    sources = ((key_own, value_own), (key_far, value_far))

    def at(i):
        j, far = divmod(i, 2)
        return j, sources[far], slice(2 * size * j, 2 * size * (j + 1)), pl.ds(far * tokens, tokens), pl.ds(i * tokens, tokens)

    def enter(i):
        j, (key, value), cols, rows, own = at(i)
        state[i, "first"] = dot(key[:, cols], const[j][1][0]).astype(BF)

    def bend(i):
        j, (key, value), cols, rows, own = at(i)
        active, slope = activate(state.pop((i, "first")), BF, True)
        active_ref[own, :] = active
        slope_ref[own, :] = slope
        state[i, "centre"] = dot(active, const[j][1][1], NT)

    def measure(i):
        centre = state[i, "centre"]
        state[i, "spread"] = averaged((centre * centre).astype(BF), mean)
        state[i, "rate"] = dot(rate_ref[at(i)[3], :], const[at(i)[0]][5])

    def compare(i):
        j, (key, value), cols, rows, own = at(i)
        _, _, gain, bias, scaled, _ = const[j]
        inverse = lax.rsqrt(state.pop((i, "spread")) + 1e-06)
        unit = state.pop((i, "centre")) * inverse
        target = value[:, cols].astype(F32) - key[:, cols].astype(F32)
        error = unit * gain + (bias - target)
        dunit = error * (state.pop((i, "rate")) * scaled)
        state[i, "along"] = averaged((dunit * unit).astype(BF), mean)
        state[i, "rest"] = (inverse, unit, dunit)

    def back(i):
        j, (key, value), cols, rows, own = at(i)
        inverse, unit, dunit = state.pop((i, "rest"))
        dsecond = (inverse * (dunit - unit * state.pop((i, "along")))).astype(BF)
        dsecond_ref[own, :] = dsecond
        state[i, "dactive"] = dot(dsecond, const[j][1][1]).astype(BF)

    def leave(i):
        j, (key, value), cols, rows, own = at(i)
        dfirst_ref[own, :] = state.pop((i, "dactive")) * slope_ref[own, :]

    def gather(i):
        j, (key, value), cols, rows, own = at(i)
        if i % 2 == 0:
            return
        base = const[j][0]
        both = pl.ds((i - 1) * tokens, 2 * tokens)
        key_t = [source[0][:, cols].T for source in sources]
        dsecond_t = dsecond_ref[both, :].T
        for head in range(2):
            part = slice(head * size, (head + 1) * size)
            lane = slice(head * width, (head + 1) * width)
            halves = [dfirst_ref[pl.ds(k * tokens, tokens), lane] for k in (i - 1, i)]
            first = dot(key_t[0][part], halves[0]) + dot(key_t[1][part], halves[1])
            second = dot(dsecond_t[part], active_ref[both, lane])
            second = second - jnp.mean(second, axis=0, keepdims=True)
            sums_ref[pl.ds(base + head * size, size), :width] = first.astype(BF)
            sums_ref[pl.ds(base + head * size, size), width:] = second.astype(BF)

    staggered((enter, bend, measure, compare, back, leave, gather), lags, 2 * pairs)

    @pl.when(step == pl.num_programs(0) - 1)
    def _():
        for rel, out in enumerate(out_refs):
            at = pl.multiple_of((mine ^ rel) * rows_own, rows_own)
            for g in range(groups):
                out[g] = sums_ref[pl.ds(g * members * rows_own + at, rows_own), :]


def vmem(x):
    return pltpu.with_memory_space_constraint(x, pltpu.VMEM)


def gradient(place, own, far, rates, weights, gain, bias, total, lag, pairs=1, lags=(0, 1, 2, 3, 4, 5, 6)):
    tokens = own[0].shape[0]
    heads, size = gain.shape
    members = len(weights)
    groups, rows_own, two = weights[0].shape
    per = members * rows_own // (2 * size)
    zof = lambda i, place: place[0] ^ (i * pairs // per + lag)
    wide = pairs * 2 * size
    own_spec = pl.BlockSpec((tokens, wide), lambda i, place: (0, ((zof(i, place) * 2 + place[1]) * per + i * pairs % per) // pairs))
    far_spec = pl.BlockSpec((tokens, wide), lambda i, place: (0, (zof(i, place) * per + i * pairs % per) // pairs))
    whole = lambda shape: pl.BlockSpec(shape, lambda i, place: (0,) * len(shape))
    mat = whole((groups, rows_own, two))
    held = pl.BlockSpec(memory_space=pltpu.VMEM)
    rows = groups * members * rows_own
    return pl.pallas_call(
        functools.partial(grad_kernel, size, lags, pairs, per, lag, total),
        out_shape=[pltpu.VMEM((groups, rows_own, two), BF)] * members,
        grid_spec=pltpu.PrefetchScalarGridSpec(
            num_scalar_prefetch=1,
            grid=(groups * per // pairs,),
            in_specs=[own_spec] * 2 + [far_spec] * 2 + [held] * (4 + members),
            out_specs=[held] * members,
            scratch_shapes=[
                pltpu.VMEM((rows, two), BF),
                pltpu.VMEM((rows, two), BF),
                pltpu.VMEM((2 * pairs * tokens, two), BF),
                pltpu.VMEM((2 * pairs * tokens, two), BF),
                pltpu.VMEM((2 * pairs * tokens, 2 * size), BF),
                pltpu.VMEM((2 * pairs * tokens, two), BF),
                pltpu.VMEM((2 * tokens, heads), BF),
            ],
        ),
        compiler_params=pltpu.CompilerParams(vmem_limit_bytes=48 << 20),
        name="fast_gradient",
    )(place, *own, *far, *map(vmem, rates), *map(vmem, weights), vmem(gain), vmem(bias))


def output_kernel(size, chunk, lags, pairs, per, lag, flip, place_ref, query_ref, weight_ref, gain_ref, bias_ref, *refs):
    out_ref, whole_ref = refs[-2:]
    step = pl.program_id(0)
    members, _, rows_own, _ = weight_ref.shape

    @pl.when(step == 0)
    def _():
        fill(whole_ref, [weight_ref.at[rel] for rel in range(members)], place_ref[2], rows_own)

    mean = head_mean(size, 4)
    zof = place_ref[0] ^ (step * pairs // per + lag)
    first_pair = (zof * 2 + (place_ref[1] ^ flip)) * per + (step * pairs) % per
    const, state = [], {}
    for j in range(pairs):
        base = pl.multiple_of((step * pairs + j) * 2 * size, 2 * size)
        const.append((blocks(whole_ref[pl.ds(base, 2 * size), :], size), pair_row(gain_ref, first_pair + j), pair_row(bias_ref, first_pair + j)))
    count = query_ref.shape[0] // chunk

    def at(i):
        j, k = divmod(i, count)
        return const[j], (pl.ds(k * chunk, chunk), slice(2 * size * j, 2 * size * (j + 1)))

    def enter(i):
        (mats, gain, bias), where = at(i)
        state[i, "first"] = dot(query_ref[where], mats[0]).astype(BF)

    def bend(i):
        (mats, gain, bias), where = at(i)
        state[i, "centre"] = dot(activate(state.pop((i, "first")), BF, False), mats[1], NT)

    def measure(i):
        centre = state[i, "centre"]
        state[i, "spread"] = averaged((centre * centre).astype(BF), mean)

    def leave(i):
        (mats, gain, bias), where = at(i)
        unit = state.pop((i, "centre")) * lax.rsqrt(state.pop((i, "spread")) + 1e-06)
        out_ref[where] = (query_ref[where].astype(F32) + unit * gain + bias).astype(BF)

    staggered((enter, bend, measure, leave), lags, pairs * count)


def output(place, queries, weights, gain, bias, before, lag, flip, pairs=1, chunk=256, lags=(0, 1, 2, 3)):
    tokens, model = queries.shape
    members, groups, rows_own, two = weights.shape
    _, size = gain.shape
    per = members * rows_own // (2 * size)
    column = lambda i, place: (((place[0] ^ (i * pairs // per + lag)) * 2 + (place[1] ^ flip)) * per + i * pairs % per) // pairs
    col = pl.BlockSpec((tokens, pairs * 2 * size), lambda i, place: (0, column(i, place)))
    more = [] if before is None else [before]
    return pl.pallas_call(
        functools.partial(output_kernel, size, chunk, lags, pairs, per, lag, flip),
        out_shape=jax.ShapeDtypeStruct((tokens, model), BF),
        grid_spec=pltpu.PrefetchScalarGridSpec(
            num_scalar_prefetch=1,
            grid=(groups * per // pairs,),
            in_specs=[col] + [pl.BlockSpec(memory_space=pltpu.VMEM)] * 3 + [pl.BlockSpec(memory_space=pl.ANY)] * len(more),
            out_specs=col,
            scratch_shapes=[pltpu.VMEM((groups * members * rows_own, two), BF)],
        ),
        input_output_aliases={5: 0} if more else {},
        compiler_params=pltpu.CompilerParams(vmem_limit_bytes=48 << 20),
        name="fast_output",
    )(place, queries, vmem(weights), vmem(gain), vmem(bias), *more)


def pick_kernel(place_ref, *refs):
    half = len(refs) // 2
    for source, target in zip(refs[:half], refs[half:]):
        target[...] = source[...]


def pick(place, arrays, groups, flip):
    tokens, model = arrays[0].shape
    wide = model // (2 * groups)
    return pl.pallas_call(
        pick_kernel,
        out_shape=[jax.ShapeDtypeStruct((tokens, groups * wide), a.dtype) for a in arrays],
        grid_spec=pltpu.PrefetchScalarGridSpec(
            num_scalar_prefetch=1,
            grid=(groups,),
            in_specs=[pl.BlockSpec((tokens, wide), lambda i, place: (0, 2 * i + (place[1] ^ flip)))] * len(arrays),
            out_specs=[pl.BlockSpec((tokens, wide), lambda i, place: (0, i))] * len(arrays),
        ),
        name="pick",
    )(place, *arrays)


def core_swap(x):
    n = lax.axis_size("gx")
    return lax.ppermute(x, "gx", [(i, i ^ 1) for i in range(n)])


def z_shift(x, s):
    n = lax.axis_size("gx")
    return lax.ppermute(x, "gx", [(i, i ^ (2 * s)) for i in range(n)])


def plane_shift(x, s):
    n = lax.axis_size("gy")
    return lax.ppermute(x, "gy", [(i, i ^ s) for i in range(n)])


def fetch(fast, groups, members, chunks):
    narrow = fast.astype(BF)
    held = [narrow]
    for s in range(1, groups):
        held.append(z_shift(narrow, s))
    weights = []
    for at, count in chunks:
        mine = jnp.stack(held[at : at + count])
        weights.append([mine])
        for s in range(1, members):
            weights[-1].append(plane_shift(mine, s))
    return weights


def collect(parts, groups, members, chunks):
    sums = {}
    for part, (at, count) in zip(parts, chunks):
        arrived = [part[0]]
        for s in range(1, members):
            arrived.append(plane_shift(part[s], s))
        for g in range(count):
            sums[at + g] = sum([a[g].astype(F32) for a in arrived])
    total = sums[0]
    for s in range(1, groups):
        total = total + z_shift(sums[s].astype(BF), s).astype(F32)
    return total


def per_device(
    key_rows, value_rows, query_rows, token_rates, fast_weights, momentum, norm_gain, norm_bias
):
    size = norm_gain.shape[1]
    groups, members = lax.axis_size("gx") // 2, lax.axis_size("gy")
    total = key_rows.shape[0] * 2 * groups * members
    gx = lax.axis_index("gx")
    place = jnp.stack([gx // 2, gx % 2, lax.axis_index("gy")]).astype(jnp.int32)
    half = groups // 2
    near, remote = (0, half), (half, groups - half)
    orders = [(near, remote)] * (STEPS + 1)
    pairs = members * fast_weights.shape[0] // (2 * size)
    pairs = pairs if pairs <= 3 else 1
    fast, moment = (fast_weights, momentum)
    weights = fetch(fast, groups, members, orders[0])
    key_send, value_send = pick(place, (key_rows, value_rows), groups, 1)
    far = (core_swap(key_send),)
    far += (core_swap(value_send),)
    own = (key_rows, value_rows)
    rates = (token_rates.T, core_swap(token_rates).T)
    for step in range(STEPS):
        parts = []
        for k, (w, (at, count)) in enumerate(zip(weights, orders[step])):
            turn = place if k == 0 else lax.optimization_barrier((place, parts[-1][0]))[0]
            parts.append(gradient(turn, own, far, rates, w, norm_gain, norm_bias, total, at, pairs))
        grad = collect(parts, groups, members, orders[step])
        moment = momentum_keep * moment + grad
        fast = fast - inner_rate * moment
        weights = fetch(fast, groups, members, orders[step + 1])
    chunk = min(512, query_rows.shape[0])
    mixed, twins = None, []
    for w, (at, count) in zip(weights, orders[STEPS]):
        if mixed is not None:
            *w, mixed = lax.optimization_barrier((*w, mixed))
        whole = jnp.stack(w)
        twins.append(core_swap(whole))
        mixed = output(place, query_rows, whole, norm_gain, norm_bias, mixed, at, 0, pairs, chunk)
    for w, (at, count) in zip(twins, orders[STEPS]):
        mixed = output(place, query_rows, w, norm_gain, norm_bias, mixed, at, 1, pairs, chunk)
    return (mixed, fast, moment)


def plain_grad_kernel(size, chunk, total, kind, key_ref, value_ref, rate_ref, packed_ref, gain_ref, bias_ref, out_ref,
                active_ref, dfirst_ref, dsecond_ref):
    tokens = key_ref.shape[0]
    width = packed_ref.shape[1] // 2
    first_w, second_w = blocks(packed_ref[...], size)
    mean = head_mean(size, 2)
    gain = gain_ref[0]
    bias = bias_ref[0]
    scaled = gain * (1.0 / total)
    for at in range(0, tokens, chunk):
        rows = pl.ds(at, chunk)
        keys = key_ref[rows, :]
        first = dot(keys, first_w)
        active, slope = activate(first, kind, True)
        active_ref[rows, :] = active
        centre = dot(active, second_w, NT)
        spread = dot((centre * centre).astype(jnp.bfloat16), mean)
        inverse = lax.rsqrt(spread + 1e-06)
        unit = centre * inverse
        target = value_ref[rows, :].astype(jnp.float32) - keys.astype(jnp.float32)
        error = unit * gain + (bias - target)
        dunit = error * (rate_ref[rows, :].astype(jnp.float32) * scaled)
        along = dot((dunit * unit).astype(jnp.bfloat16), mean)
        dsecond = (inverse * (dunit - unit * along)).astype(jnp.bfloat16)
        dsecond_ref[rows, :] = dsecond
        dactive = dot(dsecond, second_w)
        dfirst_ref[rows, :] = (dactive * slope.astype(F32)).astype(jnp.bfloat16)
    keys_t = key_ref[...].T
    dsecond_t = dsecond_ref[...].T
    for head in range(2):
        mine = slice(head * size, (head + 1) * size)
        cols = slice(head * width, (head + 1) * width)
        out_ref[mine, :width] = dot(keys_t[mine], dfirst_ref[:, cols]).astype(out_ref.dtype)
        second = dot(dsecond_t[mine], active_ref[:, cols])
        out_ref[mine, width:] = (second - jnp.mean(second, axis=0, keepdims=True)).astype(out_ref.dtype)


def plain_apply_kernel(size, chunk, kind, query_ref, packed_ref, gain_ref, bias_ref, out_ref):
    tokens = query_ref.shape[0]
    first_w, second_w = blocks(packed_ref[...], size)
    mean = head_mean(size, 2)
    gain = gain_ref[0]
    bias = bias_ref[0]
    for at in range(0, tokens, chunk):
        rows = pl.ds(at, chunk)
        queries = query_ref[rows, :]
        first = dot(queries, first_w)
        active = activate(first, kind, False)
        centre = dot(active, second_w, NT)
        spread = dot((centre * centre).astype(jnp.bfloat16), mean)
        unit = centre * lax.rsqrt(spread + 1e-06)
        out_ref[rows, :] = (queries.astype(jnp.float32) + unit * gain + bias).astype(out_ref.dtype)


def plain_gradient(keys, values, rates, packed, gain, bias, total, size, chunk=128, kind=jnp.float32):
    tokens = keys.shape[0]
    rows, two = packed.shape
    pairs = rows // (2 * size)
    col = pl.BlockSpec((tokens, 2 * size), lambda i: (0, i))
    vec = pl.BlockSpec((1, 1, 2 * size), lambda i: (i, 0, 0))
    mat = pl.BlockSpec((2 * size, two), lambda i: (i, 0))
    return pl.pallas_call(
        functools.partial(plain_grad_kernel, size, chunk, total, kind),
        out_shape=jax.ShapeDtypeStruct((rows, two), jnp.bfloat16),
        grid=(pairs,),
        in_specs=[col, col, col, mat, vec, vec],
        out_specs=mat,
        scratch_shapes=[pltpu.VMEM((tokens, two), jnp.bfloat16), pltpu.VMEM((tokens, two), jnp.bfloat16), pltpu.VMEM((tokens, 2 * size), jnp.bfloat16)],
        name="plain_gradient",
    )(keys, values, rates, packed, gain.reshape(pairs, 1, 2 * size), bias.reshape(pairs, 1, 2 * size))


def plain_output(queries, packed, gain, bias, size, chunk=128, kind=jnp.float32):
    tokens = queries.shape[0]
    rows, two = packed.shape
    pairs = rows // (2 * size)
    col = pl.BlockSpec((tokens, 2 * size), lambda i: (0, i))
    vec = pl.BlockSpec((1, 1, 2 * size), lambda i: (i, 0, 0))
    mat = pl.BlockSpec((2 * size, two), lambda i: (i, 0))
    return pl.pallas_call(
        functools.partial(plain_apply_kernel, size, chunk, kind),
        out_shape=jax.ShapeDtypeStruct((tokens, rows), jnp.bfloat16),
        grid=(pairs,),
        in_specs=[col, mat, vec, vec],
        out_specs=col,
        name="plain_output",
    )(queries, packed, gain.reshape(pairs, 1, 2 * size), bias.reshape(pairs, 1, 2 * size))


def plain_device(
    key_rows, value_rows, query_rows, token_rates, fast_weights, momentum, norm_gain, norm_bias
):
    size = norm_gain.shape[1]
    total = key_rows.shape[0] * lax.axis_size("gx") * lax.axis_size("gy")
    place = jnp.zeros((3,), jnp.int32)
    rates = jnp.repeat(token_rates.astype(BF), size, axis=1)
    fast, moment = (fast_weights, momentum)

    def whole(fast):
        inner = lax.all_gather(fast.astype(BF), "gy", axis=0, tiled=True)
        return lax.all_gather(inner, "gx", axis=0, tiled=True)

    for _ in range(STEPS):
        part = plain_gradient(key_rows, value_rows, rates, whole(fast), norm_gain, norm_bias, total, size)
        outer = lax.psum_scatter(part, "gx", scatter_dimension=0, tiled=True)
        grad = lax.psum_scatter(outer, "gy", scatter_dimension=0, tiled=True).astype(F32)
        moment = momentum_keep * moment + grad
        fast = fast - inner_rate * moment
    mixed = plain_output(query_rows, whole(fast), norm_gain, norm_bias, size)
    return (mixed, fast, moment)


def power_of_two(n):
    return n > 0 and n & (n - 1) == 0


def solution(mesh):
    rows = P(("gx", "gy"), None)
    gx, gy = mesh.shape["gx"], mesh.shape["gy"]

    def run(*args):
        rows_own = args[0].shape[1] // mesh.size
        size = args[6].shape[1]
        paired = gx % 4 == 0 and power_of_two(gx) and power_of_two(gy)
        even = rows_own % 32 == 0 and (rows_own * gy) % (2 * size) == 0
        body = per_device if paired and even else plain_device

        return jax.shard_map(
            body,
            mesh=mesh,
            in_specs=(rows,) * 6 + (P(), P()),
            out_specs=(rows,) * 3,
            check_vma=False,
        )(*args)

    return run
```

```python
import functools

import jax
import jax.numpy as jnp
from jax import lax
from jax.experimental import pallas as pl
from jax.experimental.pallas import tpu as pltpu
from jax.sharding import PartitionSpec as P


STEPS = 2

momentum_keep = 0.9
inner_rate = 0.5

GELU_SCALE = 0.7978845608028654
GELU_CUBIC = 0.044715
NT = (((1,), (1,)), ((), ()))
NN = (((1,), (0,)), ((), ()))
BF = jnp.bfloat16
F32 = jnp.float32


def dot(a, b, dims=NN):
    return lax.dot_general(a, b, dims, preferred_element_type=F32)


def blocks(packed, size):
    width = packed.shape[1] // 2
    top, low = packed[:size], packed[size:]

    def diagonal(a, b):
        a = jnp.concatenate([a, jnp.zeros_like(a)], axis=1)
        b = jnp.concatenate([jnp.zeros_like(b), b], axis=1)
        return jnp.concatenate([a, b], axis=0).astype(BF)

    def centred(a):
        a = a[:, width:].astype(F32)
        return a - jnp.mean(a, axis=0, keepdims=True)

    return diagonal(top[:, :width], low[:, :width]), diagonal(centred(top), centred(low))


def head_mean(size, heads):
    row = lax.broadcasted_iota(jnp.int32, (heads * size, heads * size), 0) // size
    col = lax.broadcasted_iota(jnp.int32, (heads * size, heads * size), 1) // size
    return jnp.where(row == col, 1.0 / size, 0.0).astype(BF)


def averaged(x, mean):
    half, wide = x.shape[0] // 2, x.shape[1]
    both = dot(jnp.concatenate([x[:half], x[half:]], axis=1), mean)
    return jnp.concatenate([both[:, :wide], both[:, wide:]], axis=0)


def pair_row(ref, pair):
    return jnp.concatenate([ref[pl.ds(2 * pair, 1), :], ref[pl.ds(2 * pair + 1, 1), :]], axis=1)


def fill(whole_ref, parts, mine, rows_own):
    for rel, part in enumerate(parts):
        at = pl.multiple_of((mine ^ rel) * rows_own, rows_own)
        for g in range(part.shape[0]):
            whole_ref[pl.ds(g * len(parts) * rows_own + at, rows_own), :] = part[g]


def staggered(stages, lags, n):
    for t in range(n + max(lags)):
        for stage, lag in sorted(zip(stages, lags), key=lambda item: -item[1]):
            if 0 <= t - lag < n:
                stage(t - lag)


def activate(first, kind, slope_too):
    const = lambda x: jnp.asarray(x, kind)
    first = first.astype(kind)
    square = first * first
    inner = first * (square * const(GELU_SCALE * GELU_CUBIC) + const(GELU_SCALE))
    half = jnp.tanh(inner) * const(0.5) + const(0.5)
    active = first * half
    if not slope_too:
        return active.astype(BF)
    poly = square * const(6 * GELU_SCALE * GELU_CUBIC) + const(2 * GELU_SCALE)
    slope = half + (active - active * half) * poly
    return active.astype(BF), slope.astype(BF)


def grad_kernel(size, lags, pairs, per, lag, total, place_ref, *refs):
    key_own, value_own, key_far, value_far, rate_own, rate_far = refs[:6]
    members = (len(refs) - 15) // 2
    weight_refs = refs[6 : 6 + members]
    gain_ref, bias_ref = refs[6 + members : 8 + members]
    out_refs = refs[8 + members : 8 + 2 * members]
    whole_ref, sums_ref, active_ref, dfirst_ref, dsecond_ref, slope_ref, rate_ref = refs[-7:]
    step = pl.program_id(0)
    mine = place_ref[2]
    groups, rows_own, two = weight_refs[0].shape
    width = two // 2
    tokens = key_own.shape[0]
    heads = rate_own.shape[0]

    @pl.when(step == 0)
    def _():
        fill(whole_ref, weight_refs, mine, rows_own)
        rate_ref[:tokens, :] = rate_own[...].T.astype(BF)
        rate_ref[tokens:, :] = rate_far[...].T.astype(BF)

    mean = head_mean(size, 4)
    head_row = lax.broadcasted_iota(jnp.int32, (heads, 2 * size), 0)
    head_col = lax.broadcasted_iota(jnp.int32, (heads, 2 * size), 1) // size
    zof = place_ref[0] ^ (step * pairs // per + lag)
    first_pair = (zof * 2 + place_ref[1]) * per + (step * pairs) % per
    const, state = [], {}
    for j in range(pairs):
        base = pl.multiple_of((step * pairs + j) * 2 * size, 2 * size)
        gain = pair_row(gain_ref, first_pair + j)
        pick = jnp.where(head_row == 2 * (first_pair + j) + head_col, 1.0, 0.0).astype(BF)
        const.append((base, blocks(whole_ref[pl.ds(base, 2 * size), :], size), gain, pair_row(bias_ref, first_pair + j), gain * (1.0 / total), pick))
    sources = ((key_own, value_own), (key_far, value_far))
    starts = (first_pair * 2 * size, (zof * per + (step * pairs) % per) * 2 * size)

    def columns(far, j):
        return pl.ds(pl.multiple_of(starts[far] + j * 2 * size, 2 * size), 2 * size)

    def at(i):
        j, far = divmod(i, 2)
        return j, sources[far], columns(far, j), pl.ds(far * tokens, tokens), pl.ds(i * tokens, tokens)

    def enter(i):
        j, (key, value), cols, rows, own = at(i)
        state[i, "first"] = dot(key[:, cols], const[j][1][0]).astype(BF)

    def bend(i):
        j, (key, value), cols, rows, own = at(i)
        active, slope = activate(state.pop((i, "first")), BF, True)
        active_ref[own, :] = active
        slope_ref[own, :] = slope
        state[i, "centre"] = dot(active, const[j][1][1], NT)

    def measure(i):
        centre = state[i, "centre"]
        state[i, "spread"] = averaged((centre * centre).astype(BF), mean)
        state[i, "rate"] = dot(rate_ref[at(i)[3], :], const[at(i)[0]][5])

    def compare(i):
        j, (key, value), cols, rows, own = at(i)
        _, _, gain, bias, scaled, _ = const[j]
        inverse = lax.rsqrt(state.pop((i, "spread")) + 1e-06)
        unit = state.pop((i, "centre")) * inverse
        target = value[:, cols].astype(F32) - key[:, cols].astype(F32)
        error = unit * gain + (bias - target)
        dunit = error * (state.pop((i, "rate")) * scaled)
        state[i, "along"] = averaged((dunit * unit).astype(BF), mean)
        state[i, "rest"] = (inverse, unit, dunit)

    def back(i):
        j, (key, value), cols, rows, own = at(i)
        inverse, unit, dunit = state.pop((i, "rest"))
        dsecond = (inverse * (dunit - unit * state.pop((i, "along")))).astype(BF)
        dsecond_ref[own, :] = dsecond
        state[i, "dactive"] = dot(dsecond, const[j][1][1]).astype(BF)

    def leave(i):
        j, (key, value), cols, rows, own = at(i)
        dfirst_ref[own, :] = state.pop((i, "dactive")) * slope_ref[own, :]

    def gather(i):
        j, (key, value), cols, rows, own = at(i)
        if i % 2 == 0:
            return
        base = const[j][0]
        both = pl.ds((i - 1) * tokens, 2 * tokens)
        key_t = [source[0][:, columns(far, j)].T for far, source in enumerate(sources)]
        dsecond_t = dsecond_ref[both, :].T
        for head in range(2):
            part = slice(head * size, (head + 1) * size)
            lane = slice(head * width, (head + 1) * width)
            halves = [dfirst_ref[pl.ds(k * tokens, tokens), lane] for k in (i - 1, i)]
            first = dot(key_t[0][part], halves[0]) + dot(key_t[1][part], halves[1])
            second = dot(dsecond_t[part], active_ref[both, lane])
            second = second - jnp.mean(second, axis=0, keepdims=True)
            sums_ref[pl.ds(base + head * size, size), :width] = first.astype(BF)
            sums_ref[pl.ds(base + head * size, size), width:] = second.astype(BF)

    staggered((enter, bend, measure, compare, back, leave, gather), lags, 2 * pairs)

    @pl.when(step == pl.num_programs(0) - 1)
    def _():
        for rel, out in enumerate(out_refs):
            at = pl.multiple_of((mine ^ rel) * rows_own, rows_own)
            for g in range(groups):
                out[g] = sums_ref[pl.ds(g * members * rows_own + at, rows_own), :]


def vmem(x):
    return pltpu.with_memory_space_constraint(x, pltpu.VMEM)


def gradient(place, own, far, rates, weights, gain, bias, total, lag, pairs=1, lags=(0, 1, 2, 3, 4, 5, 6)):
    tokens = own[0].shape[0]
    heads, size = gain.shape
    members = len(weights)
    groups, rows_own, two = weights[0].shape
    per = members * rows_own // (2 * size)
    held = pl.BlockSpec(memory_space=pltpu.VMEM)
    rows = groups * members * rows_own
    return pl.pallas_call(
        functools.partial(grad_kernel, size, lags, pairs, per, lag, total),
        out_shape=[pltpu.VMEM((groups, rows_own, two), BF)] * members,
        grid_spec=pltpu.PrefetchScalarGridSpec(
            num_scalar_prefetch=1,
            grid=(groups * per // pairs,),
            in_specs=[held] * (8 + members),
            out_specs=[held] * members,
            scratch_shapes=[
                pltpu.VMEM((rows, two), BF),
                pltpu.VMEM((rows, two), BF),
                pltpu.VMEM((2 * pairs * tokens, two), BF),
                pltpu.VMEM((2 * pairs * tokens, two), BF),
                pltpu.VMEM((2 * pairs * tokens, 2 * size), BF),
                pltpu.VMEM((2 * pairs * tokens, two), BF),
                pltpu.VMEM((2 * tokens, heads), BF),
            ],
        ),
        compiler_params=pltpu.CompilerParams(vmem_limit_bytes=40 << 20),
        name="fast_gradient",
    )(place, *map(vmem, own), *map(vmem, far), *map(vmem, rates), *map(vmem, weights), vmem(gain), vmem(bias))


def output_kernel(size, chunk, lags, pairs, per, lag, flip, place_ref, query_ref, weight_ref, gain_ref, bias_ref, *refs):
    out_ref, whole_ref = refs[-2:]
    step = pl.program_id(0)
    members, _, rows_own, _ = weight_ref.shape

    @pl.when(step == 0)
    def _():
        fill(whole_ref, [weight_ref.at[rel] for rel in range(members)], place_ref[2], rows_own)

    mean = head_mean(size, 4)
    zof = place_ref[0] ^ (step * pairs // per + lag)
    first_pair = (zof * 2 + (place_ref[1] ^ flip)) * per + (step * pairs) % per
    const, state = [], {}
    for j in range(pairs):
        base = pl.multiple_of((step * pairs + j) * 2 * size, 2 * size)
        const.append((blocks(whole_ref[pl.ds(base, 2 * size), :], size), pair_row(gain_ref, first_pair + j), pair_row(bias_ref, first_pair + j)))
    count = query_ref.shape[0] // chunk

    def at(i):
        j, k = divmod(i, count)
        start = pl.multiple_of((first_pair + j) * 2 * size, 2 * size)
        rows = pl.ds(k * chunk, chunk)
        return const[j], (rows, pl.ds(start, 2 * size)), (rows, slice(2 * size * j, 2 * size * (j + 1)))

    def enter(i):
        (mats, gain, bias), where, target = at(i)
        state[i, "first"] = dot(query_ref[where], mats[0]).astype(BF)

    def bend(i):
        (mats, gain, bias), where, target = at(i)
        state[i, "centre"] = dot(activate(state.pop((i, "first")), BF, False), mats[1], NT)

    def measure(i):
        centre = state[i, "centre"]
        state[i, "spread"] = averaged((centre * centre).astype(BF), mean)

    def leave(i):
        (mats, gain, bias), where, target = at(i)
        unit = state.pop((i, "centre")) * lax.rsqrt(state.pop((i, "spread")) + 1e-06)
        out_ref[target] = (query_ref[where].astype(F32) + unit * gain + bias).astype(BF)

    staggered((enter, bend, measure, leave), lags, pairs * count)


def output(place, queries, weights, gain, bias, before, lag, flip, pairs=1, chunk=256, lags=(0, 1, 2, 3)):
    tokens, model = queries.shape
    members, groups, rows_own, two = weights.shape
    _, size = gain.shape
    per = members * rows_own // (2 * size)
    column = lambda i, place: (((place[0] ^ (i * pairs // per + lag)) * 2 + (place[1] ^ flip)) * per + i * pairs % per) // pairs
    col = pl.BlockSpec((tokens, pairs * 2 * size), lambda i, place: (0, column(i, place)))
    more = [] if before is None else [before]
    return pl.pallas_call(
        functools.partial(output_kernel, size, chunk, lags, pairs, per, lag, flip),
        out_shape=jax.ShapeDtypeStruct((tokens, model), BF),
        grid_spec=pltpu.PrefetchScalarGridSpec(
            num_scalar_prefetch=1,
            grid=(groups * per // pairs,),
            in_specs=[pl.BlockSpec(memory_space=pltpu.VMEM)] * 4 + [pl.BlockSpec(memory_space=pl.ANY)] * len(more),
            out_specs=col,
            scratch_shapes=[pltpu.VMEM((groups * members * rows_own, two), BF)],
        ),
        input_output_aliases={5: 0} if more else {},
        compiler_params=pltpu.CompilerParams(vmem_limit_bytes=40 << 20),
        name="fast_output",
    )(place, vmem(queries), vmem(weights), vmem(gain), vmem(bias), *more)


def pick_kernel(groups, flip, place_ref, *refs):
    half = len(refs) // 2
    wide = refs[-1].shape[1] // groups
    for source, target in zip(refs[:half], refs[half:]):
        for g in range(groups):
            start = pl.multiple_of((2 * g + (place_ref[1] ^ flip)) * wide, wide)
            target[:, g * wide : (g + 1) * wide] = source[:, pl.ds(start, wide)]


def pick(place, arrays, groups, flip):
    tokens, model = arrays[0].shape
    held = pl.BlockSpec(memory_space=pltpu.VMEM)
    return pl.pallas_call(
        functools.partial(pick_kernel, groups, flip),
        out_shape=[pltpu.VMEM((tokens, model // 2), a.dtype) for a in arrays],
        grid_spec=pltpu.PrefetchScalarGridSpec(
            num_scalar_prefetch=1,
            grid=(1,),
            in_specs=[held] * len(arrays),
            out_specs=[held] * len(arrays),
        ),
        compiler_params=pltpu.CompilerParams(vmem_limit_bytes=32 << 20),
        name="pick",
    )(place, *map(vmem, arrays))


def core_swap(x):
    n = lax.axis_size("gx")
    return lax.ppermute(x, "gx", [(i, i ^ 1) for i in range(n)])


def z_shift(x, s):
    n = lax.axis_size("gx")
    return lax.ppermute(x, "gx", [(i, i ^ (2 * s)) for i in range(n)])


def plane_shift(x, s):
    n = lax.axis_size("gy")
    return lax.ppermute(x, "gy", [(i, i ^ s) for i in range(n)])


def fetch(fast, groups, members, chunks):
    narrow = fast.astype(BF)
    held = [narrow]
    for s in range(1, groups):
        held.append(z_shift(narrow, s))
    weights = []
    for at, count in chunks:
        mine = jnp.stack(held[at : at + count])
        weights.append([mine])
        for s in range(1, members):
            weights[-1].append(plane_shift(mine, s))
    return weights


def collect(parts, groups, members, chunks):
    sums = {}
    for part, (at, count) in zip(parts, chunks):
        arrived = [part[0]]
        for s in range(1, members):
            arrived.append(plane_shift(part[s], s))
        for g in range(count):
            sums[at + g] = sum([a[g].astype(F32) for a in arrived])
    total = sums[0]
    for s in range(1, groups):
        total = total + z_shift(sums[s].astype(BF), s).astype(F32)
    return total


def per_device(
    key_rows, value_rows, query_rows, token_rates, fast_weights, momentum, norm_gain, norm_bias
):
    size = norm_gain.shape[1]
    groups, members = lax.axis_size("gx") // 2, lax.axis_size("gy")
    total = key_rows.shape[0] * 2 * groups * members
    gx = lax.axis_index("gx")
    place = jnp.stack([gx // 2, gx % 2, lax.axis_index("gy")]).astype(jnp.int32)
    half = groups // 2
    near, remote = (0, half), (half, groups - half)
    orders = [(near, remote)] * (STEPS + 1)
    pairs = members * fast_weights.shape[0] // (2 * size)
    pairs = pairs if pairs <= 3 else 1
    fast, moment = (fast_weights, momentum)
    weights = fetch(fast, groups, members, orders[0])
    key_send, value_send = pick(place, (key_rows, value_rows), groups, 1)
    far = (core_swap(key_send),)
    far += (core_swap(value_send),)
    own = (key_rows, value_rows)
    rates = (token_rates.T, core_swap(token_rates).T)
    for step in range(STEPS):
        parts = []
        for k, (w, (at, count)) in enumerate(zip(weights, orders[step])):
            turn = place if k == 0 else lax.optimization_barrier((place, parts[-1][0]))[0]
            parts.append(gradient(turn, own, far, rates, w, norm_gain, norm_bias, total, at, pairs))
        grad = collect(parts, groups, members, orders[step])
        moment = momentum_keep * moment + grad
        fast = fast - inner_rate * moment
        weights = fetch(fast, groups, members, orders[step + 1])
    chunk = min(512, query_rows.shape[0])
    mixed, twins = None, []
    for w, (at, count) in zip(weights, orders[STEPS]):
        if mixed is not None:
            *w, mixed = lax.optimization_barrier((*w, mixed))
        whole = jnp.stack(w)
        twins.append(core_swap(whole))
        mixed = output(place, query_rows, whole, norm_gain, norm_bias, mixed, at, 0, pairs, chunk)
    for w, (at, count) in zip(twins, orders[STEPS]):
        mixed = output(place, query_rows, w, norm_gain, norm_bias, mixed, at, 1, pairs, chunk)
    return (mixed, fast, moment)


def plain_grad_kernel(size, chunk, total, kind, key_ref, value_ref, rate_ref, packed_ref, gain_ref, bias_ref, out_ref,
                active_ref, dfirst_ref, dsecond_ref):
    tokens = key_ref.shape[0]
    width = packed_ref.shape[1] // 2
    first_w, second_w = blocks(packed_ref[...], size)
    mean = head_mean(size, 2)
    gain = gain_ref[0]
    bias = bias_ref[0]
    scaled = gain * (1.0 / total)
    for at in range(0, tokens, chunk):
        rows = pl.ds(at, chunk)
        keys = key_ref[rows, :]
        first = dot(keys, first_w)
        active, slope = activate(first, kind, True)
        active_ref[rows, :] = active
        centre = dot(active, second_w, NT)
        spread = dot((centre * centre).astype(jnp.bfloat16), mean)
        inverse = lax.rsqrt(spread + 1e-06)
        unit = centre * inverse
        target = value_ref[rows, :].astype(jnp.float32) - keys.astype(jnp.float32)
        error = unit * gain + (bias - target)
        dunit = error * (rate_ref[rows, :].astype(jnp.float32) * scaled)
        along = dot((dunit * unit).astype(jnp.bfloat16), mean)
        dsecond = (inverse * (dunit - unit * along)).astype(jnp.bfloat16)
        dsecond_ref[rows, :] = dsecond
        dactive = dot(dsecond, second_w)
        dfirst_ref[rows, :] = (dactive * slope.astype(F32)).astype(jnp.bfloat16)
    keys_t = key_ref[...].T
    dsecond_t = dsecond_ref[...].T
    for head in range(2):
        mine = slice(head * size, (head + 1) * size)
        cols = slice(head * width, (head + 1) * width)
        out_ref[mine, :width] = dot(keys_t[mine], dfirst_ref[:, cols]).astype(out_ref.dtype)
        second = dot(dsecond_t[mine], active_ref[:, cols])
        out_ref[mine, width:] = (second - jnp.mean(second, axis=0, keepdims=True)).astype(out_ref.dtype)


def plain_apply_kernel(size, chunk, kind, query_ref, packed_ref, gain_ref, bias_ref, out_ref):
    tokens = query_ref.shape[0]
    first_w, second_w = blocks(packed_ref[...], size)
    mean = head_mean(size, 2)
    gain = gain_ref[0]
    bias = bias_ref[0]
    for at in range(0, tokens, chunk):
        rows = pl.ds(at, chunk)
        queries = query_ref[rows, :]
        first = dot(queries, first_w)
        active = activate(first, kind, False)
        centre = dot(active, second_w, NT)
        spread = dot((centre * centre).astype(jnp.bfloat16), mean)
        unit = centre * lax.rsqrt(spread + 1e-06)
        out_ref[rows, :] = (queries.astype(jnp.float32) + unit * gain + bias).astype(out_ref.dtype)


def plain_gradient(keys, values, rates, packed, gain, bias, total, size, chunk=128, kind=jnp.float32):
    tokens = keys.shape[0]
    rows, two = packed.shape
    pairs = rows // (2 * size)
    col = pl.BlockSpec((tokens, 2 * size), lambda i: (0, i))
    vec = pl.BlockSpec((1, 1, 2 * size), lambda i: (i, 0, 0))
    mat = pl.BlockSpec((2 * size, two), lambda i: (i, 0))
    return pl.pallas_call(
        functools.partial(plain_grad_kernel, size, chunk, total, kind),
        out_shape=jax.ShapeDtypeStruct((rows, two), jnp.bfloat16),
        grid=(pairs,),
        in_specs=[col, col, col, mat, vec, vec],
        out_specs=mat,
        scratch_shapes=[pltpu.VMEM((tokens, two), jnp.bfloat16), pltpu.VMEM((tokens, two), jnp.bfloat16), pltpu.VMEM((tokens, 2 * size), jnp.bfloat16)],
        name="plain_gradient",
    )(keys, values, rates, packed, gain.reshape(pairs, 1, 2 * size), bias.reshape(pairs, 1, 2 * size))


def plain_output(queries, packed, gain, bias, size, chunk=128, kind=jnp.float32):
    tokens = queries.shape[0]
    rows, two = packed.shape
    pairs = rows // (2 * size)
    col = pl.BlockSpec((tokens, 2 * size), lambda i: (0, i))
    vec = pl.BlockSpec((1, 1, 2 * size), lambda i: (i, 0, 0))
    mat = pl.BlockSpec((2 * size, two), lambda i: (i, 0))
    return pl.pallas_call(
        functools.partial(plain_apply_kernel, size, chunk, kind),
        out_shape=jax.ShapeDtypeStruct((tokens, rows), jnp.bfloat16),
        grid=(pairs,),
        in_specs=[col, mat, vec, vec],
        out_specs=col,
        name="plain_output",
    )(queries, packed, gain.reshape(pairs, 1, 2 * size), bias.reshape(pairs, 1, 2 * size))


def plain_device(
    key_rows, value_rows, query_rows, token_rates, fast_weights, momentum, norm_gain, norm_bias
):
    size = norm_gain.shape[1]
    total = key_rows.shape[0] * lax.axis_size("gx") * lax.axis_size("gy")
    place = jnp.zeros((3,), jnp.int32)
    rates = jnp.repeat(token_rates.astype(BF), size, axis=1)
    fast, moment = (fast_weights, momentum)

    def whole(fast):
        inner = lax.all_gather(fast.astype(BF), "gy", axis=0, tiled=True)
        return lax.all_gather(inner, "gx", axis=0, tiled=True)

    for _ in range(STEPS):
        part = plain_gradient(key_rows, value_rows, rates, whole(fast), norm_gain, norm_bias, total, size)
        outer = lax.psum_scatter(part, "gx", scatter_dimension=0, tiled=True)
        grad = lax.psum_scatter(outer, "gy", scatter_dimension=0, tiled=True).astype(F32)
        moment = momentum_keep * moment + grad
        fast = fast - inner_rate * moment
    mixed = plain_output(query_rows, whole(fast), norm_gain, norm_bias, size)
    return (mixed, fast, moment)


def power_of_two(n):
    return n > 0 and n & (n - 1) == 0


def solution(mesh):
    rows = P(("gx", "gy"), None)
    gx, gy = mesh.shape["gx"], mesh.shape["gy"]

    def run(*args):
        rows_own = args[0].shape[1] // mesh.size
        size = args[6].shape[1]
        paired = gx % 4 == 0 and power_of_two(gx) and power_of_two(gy)
        even = rows_own % 32 == 0 and (rows_own * gy) % (2 * size) == 0
        body = per_device if paired and even else plain_device

        return jax.shard_map(
            body,
            mesh=mesh,
            in_specs=(rows,) * 6 + (P(), P()),
            out_specs=(rows,) * 3,
            check_vma=False,
        )(*args)

    return run
```

```python
import functools

import jax
import jax.numpy as jnp
from jax import lax
from jax.experimental import pallas as pl
from jax.experimental.pallas import tpu as pltpu
from jax.sharding import PartitionSpec as P


STEPS = 2

momentum_keep = 0.9
inner_rate = 0.5

GELU_SCALE = 0.7978845608028654
GELU_CUBIC = 0.044715
NT = (((1,), (1,)), ((), ()))
NN = (((1,), (0,)), ((), ()))
BF = jnp.bfloat16
F32 = jnp.float32


def dot(a, b, dims=NN):
    return lax.dot_general(a, b, dims, preferred_element_type=F32)


def blocks(packed, size):
    width = packed.shape[1] // 2
    top, low = packed[:size], packed[size:]

    def diagonal(a, b):
        a = jnp.concatenate([a, jnp.zeros_like(a)], axis=1)
        b = jnp.concatenate([jnp.zeros_like(b), b], axis=1)
        return jnp.concatenate([a, b], axis=0).astype(BF)

    def centred(a):
        a = a[:, width:].astype(F32)
        return a - jnp.mean(a, axis=0, keepdims=True)

    return diagonal(top[:, :width], low[:, :width]), diagonal(centred(top), centred(low))


def head_mean(size, heads):
    row = lax.broadcasted_iota(jnp.int32, (heads * size, heads * size), 0) // size
    col = lax.broadcasted_iota(jnp.int32, (heads * size, heads * size), 1) // size
    return jnp.where(row == col, 1.0 / size, 0.0).astype(BF)


def averaged(x, mean):
    half, wide = x.shape[0] // 2, x.shape[1]
    both = dot(jnp.concatenate([x[:half], x[half:]], axis=1), mean)
    return jnp.concatenate([both[:, :wide], both[:, wide:]], axis=0)


def pair_row(ref, pair):
    return jnp.concatenate([ref[pl.ds(2 * pair, 1), :], ref[pl.ds(2 * pair + 1, 1), :]], axis=1)


def fill(whole_ref, parts, mine, rows_own):
    for rel, part in enumerate(parts):
        at = pl.multiple_of((mine ^ rel) * rows_own, rows_own)
        for g in range(part.shape[0]):
            whole_ref[pl.ds(g * len(parts) * rows_own + at, rows_own), :] = part[g]


def staggered(stages, lags, n):
    for t in range(n + max(lags)):
        for stage, lag in sorted(zip(stages, lags), key=lambda item: -item[1]):
            if 0 <= t - lag < n:
                stage(t - lag)


def activate(first, kind, slope_too):
    const = lambda x: jnp.asarray(x, kind)
    first = first.astype(kind)
    square = first * first
    inner = first * (square * const(GELU_SCALE * GELU_CUBIC) + const(GELU_SCALE))
    half = jnp.tanh(inner) * const(0.5) + const(0.5)
    active = first * half
    if not slope_too:
        return active.astype(BF)
    poly = square * const(6 * GELU_SCALE * GELU_CUBIC) + const(2 * GELU_SCALE)
    slope = half + (active - active * half) * poly
    return active.astype(BF), slope.astype(BF)


def grad_kernel(size, lags, pairs, per, lag, total, place_ref, *refs):
    key_own, value_own, key_far, value_far, rate_own, rate_far = refs[:6]
    members = (len(refs) - 15) // 2
    weight_refs = refs[6 : 6 + members]
    gain_ref, bias_ref = refs[6 + members : 8 + members]
    out_refs = refs[8 + members : 8 + 2 * members]
    whole_ref, sums_ref, active_ref, dfirst_ref, dsecond_ref, slope_ref, rate_ref = refs[-7:]
    step = pl.program_id(0)
    mine = place_ref[2]
    groups, rows_own, two = weight_refs[0].shape
    width = two // 2
    tokens = key_own.shape[0]
    heads = rate_own.shape[0]

    @pl.when(step == 0)
    def _():
        fill(whole_ref, weight_refs, mine, rows_own)
        rate_ref[...] = jnp.zeros_like(rate_ref)
        rate_ref[:tokens, :heads] = rate_own[...].T.astype(BF)
        rate_ref[tokens:, :heads] = rate_far[...].T.astype(BF)

    mean = head_mean(size, 4)
    lanes = 2 * size
    block_row = lax.broadcasted_iota(jnp.int32, (lanes + rate_ref.shape[1], 2 * lanes), 0)
    block_col = lax.broadcasted_iota(jnp.int32, (lanes + rate_ref.shape[1], 2 * lanes), 1)
    same = (block_row // size == block_col // size) & (block_row < lanes)
    zof = place_ref[0] ^ (lag[0] + lag[1] * (step * pairs // per))
    first_pair = (zof * 2 + place_ref[1]) * per + (step * pairs) % per
    const, state = [], {}
    for j in range(pairs):
        base = pl.multiple_of((step * pairs + j) * 2 * size, 2 * size)
        gain = pair_row(gain_ref, first_pair + j)
        chosen = (block_col >= lanes) & (block_row - lanes == 2 * (first_pair + j) + (block_col - lanes) // size)
        pick = jnp.where(same, 1.0 / size, jnp.where(chosen, 1.0, 0.0)).astype(BF)
        const.append((base, blocks(whole_ref[pl.ds(base, 2 * size), :], size), gain, pair_row(bias_ref, first_pair + j), gain * (1.0 / total), pick))
    sources = ((key_own, value_own), (key_far, value_far))
    starts = (first_pair * 2 * size, (zof * per + (step * pairs) % per) * 2 * size)

    def columns(far, j):
        return pl.ds(pl.multiple_of(starts[far] + j * 2 * size, 2 * size), 2 * size)

    def at(i):
        j, far = divmod(i, 2)
        return j, sources[far], columns(far, j), pl.ds(far * tokens, tokens), pl.ds(i * tokens, tokens)

    def enter(i):
        j, (key, value), cols, rows, own = at(i)
        state[i, "first"] = dot(key[:, cols], const[j][1][0]).astype(BF)

    def bend(i):
        j, (key, value), cols, rows, own = at(i)
        active, slope = activate(state.pop((i, "first")), BF, True)
        active_ref[own, :] = active
        slope_ref[own, :] = slope
        state[i, "centre"] = dot(active, const[j][1][1], NT)

    def measure(i):
        centre = state[i, "centre"]
        j, (key, value), cols, rows, own = at(i)
        both = dot(jnp.concatenate([(centre * centre).astype(BF), rate_ref[rows, :]], axis=1), const[j][5])
        state[i, "spread"], state[i, "rate"] = both[:, : 2 * size], both[:, 2 * size :]

    def compare(i):
        j, (key, value), cols, rows, own = at(i)
        _, _, gain, bias, scaled, _ = const[j]
        inverse = lax.rsqrt(state.pop((i, "spread")) + 1e-06)
        unit = state.pop((i, "centre")) * inverse
        target = value[:, cols].astype(F32) - key[:, cols].astype(F32)
        error = unit * gain + (bias - target)
        dunit = error * (state.pop((i, "rate")) * scaled)
        state[i, "along"] = averaged((dunit * unit).astype(BF), mean)
        state[i, "rest"] = (inverse, unit, dunit)

    def back(i):
        j, (key, value), cols, rows, own = at(i)
        inverse, unit, dunit = state.pop((i, "rest"))
        dsecond = (inverse * (dunit - unit * state.pop((i, "along")))).astype(BF)
        dsecond_ref[own, :] = dsecond
        state[i, "dactive"] = dot(dsecond, const[j][1][1]).astype(BF)

    def leave(i):
        j, (key, value), cols, rows, own = at(i)
        dfirst_ref[own, :] = state.pop((i, "dactive")) * slope_ref[own, :]

    def gather(i):
        j, (key, value), cols, rows, own = at(i)
        if i % 2 == 0:
            return
        base = const[j][0]
        both = pl.ds((i - 1) * tokens, 2 * tokens)
        key_t = [source[0][:, columns(far, j)].T for far, source in enumerate(sources)]
        dsecond_t = dsecond_ref[both, :].T
        for head in range(2):
            part = slice(head * size, (head + 1) * size)
            lane = slice(head * width, (head + 1) * width)
            halves = [dfirst_ref[pl.ds(k * tokens, tokens), lane] for k in (i - 1, i)]
            first = dot(key_t[0][part], halves[0]) + dot(key_t[1][part], halves[1])
            second = dot(dsecond_t[part], active_ref[both, lane])
            second = second - jnp.mean(second, axis=0, keepdims=True)
            sums_ref[pl.ds(base + head * size, size), :width] = first.astype(BF)
            sums_ref[pl.ds(base + head * size, size), width:] = second.astype(BF)

    staggered((enter, bend, measure, compare, back, leave, gather), lags, 2 * pairs)

    @pl.when(step == pl.num_programs(0) - 1)
    def _():
        for rel, out in enumerate(out_refs):
            at = pl.multiple_of((mine ^ rel) * rows_own, rows_own)
            for g in range(groups):
                out[g] = sums_ref[pl.ds(g * members * rows_own + at, rows_own), :]


def vmem(x):
    return pltpu.with_memory_space_constraint(x, pltpu.VMEM)


def gradient(place, own, far, rates, weights, gain, bias, total, lag, pairs=1, lags=(0, 1, 2, 3, 5, 6, 7)):
    tokens = own[0].shape[0]
    heads, size = gain.shape
    members = len(weights)
    groups, rows_own, two = weights[0].shape
    per = members * rows_own // (2 * size)
    held = pl.BlockSpec(memory_space=pltpu.VMEM)
    rows = groups * members * rows_own
    return pl.pallas_call(
        functools.partial(grad_kernel, size, lags, pairs, per, lag, total),
        out_shape=[pltpu.VMEM((groups, rows_own, two), BF)] * members,
        grid_spec=pltpu.PrefetchScalarGridSpec(
            num_scalar_prefetch=1,
            grid=(groups * per // pairs,),
            in_specs=[held] * (8 + members),
            out_specs=[held] * members,
            scratch_shapes=[
                pltpu.VMEM((rows, two), BF),
                pltpu.VMEM((rows, two), BF),
                pltpu.VMEM((2 * pairs * tokens, two), BF),
                pltpu.VMEM((2 * pairs * tokens, two), BF),
                pltpu.VMEM((2 * pairs * tokens, 2 * size), BF),
                pltpu.VMEM((2 * pairs * tokens, two), BF),
                pltpu.VMEM((2 * tokens, -(-heads // 128) * 128), BF),
            ],
        ),
        compiler_params=pltpu.CompilerParams(vmem_limit_bytes=40 << 20),
        name="fast_gradient",
    )(place, *map(vmem, own), *map(vmem, far), *map(vmem, rates), *map(vmem, weights), vmem(gain), vmem(bias))


def output_kernel(size, chunk, lags, pairs, per, lag, flip, place_ref, query_ref, weight_ref, gain_ref, bias_ref, *refs):
    out_ref, whole_ref = refs[-2:]
    step = pl.program_id(0)
    members, _, rows_own, _ = weight_ref.shape

    @pl.when(step == 0)
    def _():
        fill(whole_ref, [weight_ref.at[rel] for rel in range(members)], place_ref[2], rows_own)

    mean = head_mean(size, 4)
    zof = place_ref[0] ^ (lag[0] + lag[1] * (step * pairs // per))
    first_pair = (zof * 2 + (place_ref[1] ^ flip)) * per + (step * pairs) % per
    const, state = [], {}
    for j in range(pairs):
        base = pl.multiple_of((step * pairs + j) * 2 * size, 2 * size)
        const.append((blocks(whole_ref[pl.ds(base, 2 * size), :], size), pair_row(gain_ref, first_pair + j), pair_row(bias_ref, first_pair + j)))
    count = query_ref.shape[0] // chunk

    def at(i):
        j, k = divmod(i, count)
        start = pl.multiple_of((first_pair + j) * 2 * size, 2 * size)
        rows = pl.ds(k * chunk, chunk)
        return const[j], (rows, pl.ds(start, 2 * size)), (rows, slice(2 * size * j, 2 * size * (j + 1)))

    def enter(i):
        (mats, gain, bias), where, target = at(i)
        state[i, "first"] = dot(query_ref[where], mats[0]).astype(BF)

    def bend(i):
        (mats, gain, bias), where, target = at(i)
        state[i, "centre"] = dot(activate(state.pop((i, "first")), BF, False), mats[1], NT)

    def measure(i):
        centre = state[i, "centre"]
        state[i, "spread"] = averaged((centre * centre).astype(BF), mean)

    def leave(i):
        (mats, gain, bias), where, target = at(i)
        unit = state.pop((i, "centre")) * lax.rsqrt(state.pop((i, "spread")) + 1e-06)
        out_ref[target] = (query_ref[where].astype(F32) + unit * gain + bias).astype(BF)

    staggered((enter, bend, measure, leave), lags, pairs * count)


def output(place, queries, weights, gain, bias, before, lag, flip, pairs=1, chunk=256, lags=(0, 1, 2, 3)):
    tokens, model = queries.shape
    members, groups, rows_own, two = weights.shape
    _, size = gain.shape
    per = members * rows_own // (2 * size)
    column = lambda i, place: (((place[0] ^ (lag[0] + lag[1] * (i * pairs // per))) * 2 + (place[1] ^ flip)) * per + i * pairs % per) // pairs
    col = pl.BlockSpec((tokens, pairs * 2 * size), lambda i, place: (0, column(i, place)))
    more = [] if before is None else [before]
    return pl.pallas_call(
        functools.partial(output_kernel, size, chunk, lags, pairs, per, lag, flip),
        out_shape=jax.ShapeDtypeStruct((tokens, model), BF),
        grid_spec=pltpu.PrefetchScalarGridSpec(
            num_scalar_prefetch=1,
            grid=(groups * per // pairs,),
            in_specs=[pl.BlockSpec(memory_space=pltpu.VMEM)] * 4 + [pl.BlockSpec(memory_space=pl.ANY)] * len(more),
            out_specs=col,
            scratch_shapes=[pltpu.VMEM((groups * members * rows_own, two), BF)],
        ),
        input_output_aliases={5: 0} if more else {},
        compiler_params=pltpu.CompilerParams(vmem_limit_bytes=40 << 20),
        name="fast_output",
    )(place, vmem(queries), vmem(weights), vmem(gain), vmem(bias), *more)


def pick_kernel(groups, flip, place_ref, *refs):
    half = (len(refs) - 1) // 2
    sems = refs[-1]
    wide = refs[half].shape[1] // groups
    copies = []
    for k in range(half):
        for g in range(groups):
            start = pl.multiple_of((2 * g + (place_ref[1] ^ flip)) * wide, wide)
            target = refs[half + k].at[:, g * wide : (g + 1) * wide]
            copies.append(pltpu.make_async_copy(refs[k].at[:, pl.ds(start, wide)], target, sems.at[k, g]))
    for copy in copies:
        copy.start()
    for copy in copies:
        copy.wait()


def pick(place, arrays, groups, flip):
    tokens, model = arrays[0].shape
    return pl.pallas_call(
        functools.partial(pick_kernel, groups, flip),
        out_shape=[pltpu.VMEM((tokens, model // 2), a.dtype) for a in arrays],
        grid_spec=pltpu.PrefetchScalarGridSpec(
            num_scalar_prefetch=1,
            grid=(1,),
            in_specs=[pl.BlockSpec(memory_space=pltpu.HBM)] * len(arrays),
            out_specs=[pl.BlockSpec(memory_space=pltpu.VMEM)] * len(arrays),
            scratch_shapes=[pltpu.SemaphoreType.DMA((len(arrays), groups))],
        ),
        compiler_params=pltpu.CompilerParams(vmem_limit_bytes=32 << 20),
        name="pick",
    )(place, *[pltpu.with_memory_space_constraint(x, pltpu.HBM) for x in arrays])


def core_swap(x):
    n = lax.axis_size("gx")
    return lax.ppermute(x, "gx", [(i, i ^ 1) for i in range(n)])


def z_shift(x, s):
    n = lax.axis_size("gx")
    return lax.ppermute(x, "gx", [(i, i ^ (2 * s)) for i in range(n)])


def plane_shift(x, s):
    n = lax.axis_size("gy")
    return lax.ppermute(x, "gy", [(i, i ^ s) for i in range(n)])


def fetch(fast, groups, members, chunks):
    narrow = lax.optimization_barrier(fast.astype(BF))
    held = [narrow]
    for s in range(1, groups):
        held.append(z_shift(narrow, s))
    weights = []
    for at, stride in chunks:
        mine = jnp.stack([held[at + stride * g] for g in range(groups // 2)])
        weights.append([mine])
        for s in range(1, members):
            weights[-1].append(plane_shift(mine, s))
    return weights


def collect(parts, groups, members, chunks):
    sums = {}
    for part, (at, stride) in zip(parts, chunks):
        arrived = [part[0]]
        for s in range(1, members):
            arrived.append(plane_shift(part[s], s))
        for g in range(groups // 2):
            sums[at + stride * g] = sum([a[g].astype(F32) for a in arrived])
    total = sums[0]
    for s in range(1, groups):
        total = total + z_shift(sums[s].astype(BF), s).astype(F32)
    return total


def per_device(
    key_rows, value_rows, query_rows, token_rates, fast_weights, momentum, norm_gain, norm_bias
):
    size = norm_gain.shape[1]
    groups, members = lax.axis_size("gx") // 2, lax.axis_size("gy")
    total = key_rows.shape[0] * 2 * groups * members
    gx = lax.axis_index("gx")
    place = jnp.stack([gx // 2, gx % 2, lax.axis_index("gy")]).astype(jnp.int32)
    evens, odds = (0, 2), (1, 2)
    orders = [(evens, odds)] * STEPS + [((0, 1), (groups // 2, 1))]
    pairs = members * fast_weights.shape[0] // (2 * size)
    pairs = pairs if pairs <= 3 else 1
    fast, moment = (fast_weights, momentum)
    weights = fetch(fast, groups, members, orders[0])
    key_send, value_send = pick(place, (key_rows, value_rows), groups, 1)
    far = (core_swap(key_send),)
    far += (core_swap(value_send),)
    own = (key_rows, value_rows)
    rates = (token_rates.T, core_swap(token_rates).T)
    for step in range(STEPS):
        parts = []
        for k, (w, at) in enumerate(zip(weights, orders[step])):
            turn = place if k == 0 else lax.optimization_barrier((place, parts[-1][0]))[0]
            parts.append(gradient(turn, own, far, rates, w, norm_gain, norm_bias, total, at, pairs))
        grad = collect(parts, groups, members, orders[step])
        moment = momentum_keep * moment + grad
        fast = fast - inner_rate * moment
        weights = fetch(fast, groups, members, orders[step + 1])
    chunk = min(512, query_rows.shape[0])
    mixed, twins = None, []
    for w, at in zip(weights, orders[STEPS]):
        if mixed is not None:
            *w, mixed = lax.optimization_barrier((*w, mixed))
        whole = jnp.stack(w)
        twins.append(core_swap(whole))
        mixed = output(place, query_rows, whole, norm_gain, norm_bias, mixed, at, 0, pairs, chunk)
    for w, at in zip(twins, orders[STEPS]):
        mixed = output(place, query_rows, w, norm_gain, norm_bias, mixed, at, 1, pairs, chunk)
    return (mixed, fast, moment)


def plain_grad_kernel(size, chunk, total, kind, key_ref, value_ref, rate_ref, packed_ref, gain_ref, bias_ref, out_ref,
                active_ref, dfirst_ref, dsecond_ref):
    tokens = key_ref.shape[0]
    width = packed_ref.shape[1] // 2
    first_w, second_w = blocks(packed_ref[...], size)
    mean = head_mean(size, 2)
    gain = gain_ref[0]
    bias = bias_ref[0]
    scaled = gain * (1.0 / total)
    for at in range(0, tokens, chunk):
        rows = pl.ds(at, chunk)
        keys = key_ref[rows, :]
        first = dot(keys, first_w)
        active, slope = activate(first, kind, True)
        active_ref[rows, :] = active
        centre = dot(active, second_w, NT)
        spread = dot((centre * centre).astype(jnp.bfloat16), mean)
        inverse = lax.rsqrt(spread + 1e-06)
        unit = centre * inverse
        target = value_ref[rows, :].astype(jnp.float32) - keys.astype(jnp.float32)
        error = unit * gain + (bias - target)
        dunit = error * (rate_ref[rows, :].astype(jnp.float32) * scaled)
        along = dot((dunit * unit).astype(jnp.bfloat16), mean)
        dsecond = (inverse * (dunit - unit * along)).astype(jnp.bfloat16)
        dsecond_ref[rows, :] = dsecond
        dactive = dot(dsecond, second_w)
        dfirst_ref[rows, :] = (dactive * slope.astype(F32)).astype(jnp.bfloat16)
    keys_t = key_ref[...].T
    dsecond_t = dsecond_ref[...].T
    for head in range(2):
        mine = slice(head * size, (head + 1) * size)
        cols = slice(head * width, (head + 1) * width)
        out_ref[mine, :width] = dot(keys_t[mine], dfirst_ref[:, cols]).astype(out_ref.dtype)
        second = dot(dsecond_t[mine], active_ref[:, cols])
        out_ref[mine, width:] = (second - jnp.mean(second, axis=0, keepdims=True)).astype(out_ref.dtype)


def plain_apply_kernel(size, chunk, kind, query_ref, packed_ref, gain_ref, bias_ref, out_ref):
    tokens = query_ref.shape[0]
    first_w, second_w = blocks(packed_ref[...], size)
    mean = head_mean(size, 2)
    gain = gain_ref[0]
    bias = bias_ref[0]
    for at in range(0, tokens, chunk):
        rows = pl.ds(at, chunk)
        queries = query_ref[rows, :]
        first = dot(queries, first_w)
        active = activate(first, kind, False)
        centre = dot(active, second_w, NT)
        spread = dot((centre * centre).astype(jnp.bfloat16), mean)
        unit = centre * lax.rsqrt(spread + 1e-06)
        out_ref[rows, :] = (queries.astype(jnp.float32) + unit * gain + bias).astype(out_ref.dtype)


def plain_gradient(keys, values, rates, packed, gain, bias, total, size, chunk=128, kind=jnp.float32):
    tokens = keys.shape[0]
    rows, two = packed.shape
    pairs = rows // (2 * size)
    col = pl.BlockSpec((tokens, 2 * size), lambda i: (0, i))
    vec = pl.BlockSpec((1, 1, 2 * size), lambda i: (i, 0, 0))
    mat = pl.BlockSpec((2 * size, two), lambda i: (i, 0))
    return pl.pallas_call(
        functools.partial(plain_grad_kernel, size, chunk, total, kind),
        out_shape=jax.ShapeDtypeStruct((rows, two), jnp.bfloat16),
        grid=(pairs,),
        in_specs=[col, col, col, mat, vec, vec],
        out_specs=mat,
        scratch_shapes=[pltpu.VMEM((tokens, two), jnp.bfloat16), pltpu.VMEM((tokens, two), jnp.bfloat16), pltpu.VMEM((tokens, 2 * size), jnp.bfloat16)],
        name="plain_gradient",
    )(keys, values, rates, packed, gain.reshape(pairs, 1, 2 * size), bias.reshape(pairs, 1, 2 * size))


def plain_output(queries, packed, gain, bias, size, chunk=128, kind=jnp.float32):
    tokens = queries.shape[0]
    rows, two = packed.shape
    pairs = rows // (2 * size)
    col = pl.BlockSpec((tokens, 2 * size), lambda i: (0, i))
    vec = pl.BlockSpec((1, 1, 2 * size), lambda i: (i, 0, 0))
    mat = pl.BlockSpec((2 * size, two), lambda i: (i, 0))
    return pl.pallas_call(
        functools.partial(plain_apply_kernel, size, chunk, kind),
        out_shape=jax.ShapeDtypeStruct((tokens, rows), jnp.bfloat16),
        grid=(pairs,),
        in_specs=[col, mat, vec, vec],
        out_specs=col,
        name="plain_output",
    )(queries, packed, gain.reshape(pairs, 1, 2 * size), bias.reshape(pairs, 1, 2 * size))


def plain_device(
    key_rows, value_rows, query_rows, token_rates, fast_weights, momentum, norm_gain, norm_bias
):
    size = norm_gain.shape[1]
    total = key_rows.shape[0] * lax.axis_size("gx") * lax.axis_size("gy")
    place = jnp.zeros((3,), jnp.int32)
    rates = jnp.repeat(token_rates.astype(BF), size, axis=1)
    fast, moment = (fast_weights, momentum)

    def whole(fast):
        inner = lax.all_gather(fast.astype(BF), "gy", axis=0, tiled=True)
        return lax.all_gather(inner, "gx", axis=0, tiled=True)

    for _ in range(STEPS):
        part = plain_gradient(key_rows, value_rows, rates, whole(fast), norm_gain, norm_bias, total, size)
        outer = lax.psum_scatter(part, "gx", scatter_dimension=0, tiled=True)
        grad = lax.psum_scatter(outer, "gy", scatter_dimension=0, tiled=True).astype(F32)
        moment = momentum_keep * moment + grad
        fast = fast - inner_rate * moment
    mixed = plain_output(query_rows, whole(fast), norm_gain, norm_bias, size)
    return (mixed, fast, moment)


def power_of_two(n):
    return n > 0 and n & (n - 1) == 0


def solution(mesh):
    rows = P(("gx", "gy"), None)
    gx, gy = mesh.shape["gx"], mesh.shape["gy"]

    def run(*args):
        rows_own = args[0].shape[1] // mesh.size
        size = args[6].shape[1]
        paired = gx % 4 == 0 and power_of_two(gx) and power_of_two(gy)
        even = rows_own % 32 == 0 and (rows_own * gy) % (2 * size) == 0
        body = per_device if paired and even else plain_device

        return jax.shard_map(
            body,
            mesh=mesh,
            in_specs=(rows,) * 6 + (P(), P()),
            out_specs=(rows,) * 3,
            check_vma=False,
        )(*args)

    return run
```

```python
import functools

import jax
import jax.numpy as jnp
from jax import lax
from jax.experimental import pallas as pl
from jax.experimental.pallas import tpu as pltpu
from jax.sharding import PartitionSpec as P


STEPS = 2

momentum_keep = 0.9
inner_rate = 0.5

GELU_SCALE = 0.7978845608028654
GELU_CUBIC = 0.044715
NT = (((1,), (1,)), ((), ()))
NN = (((1,), (0,)), ((), ()))
BF = jnp.bfloat16
F32 = jnp.float32


def dot(a, b, dims=NN):
    return lax.dot_general(a, b, dims, preferred_element_type=F32)


def blocks(packed, size):
    width = packed.shape[1] // 2
    top, low = packed[:size], packed[size:]

    def diagonal(a, b):
        a = jnp.concatenate([a, jnp.zeros_like(a)], axis=1)
        b = jnp.concatenate([jnp.zeros_like(b), b], axis=1)
        return jnp.concatenate([a, b], axis=0).astype(BF)

    def centred(a):
        a = a[:, width:].astype(F32)
        return a - jnp.mean(a, axis=0, keepdims=True)

    return diagonal(top[:, :width], low[:, :width]), diagonal(centred(top), centred(low))


def head_mean(size, heads):
    row = lax.broadcasted_iota(jnp.int32, (heads * size, heads * size), 0) // size
    col = lax.broadcasted_iota(jnp.int32, (heads * size, heads * size), 1) // size
    return jnp.where(row == col, 1.0 / size, 0.0).astype(BF)


def averaged(x, mean):
    half, wide = x.shape[0] // 2, x.shape[1]
    both = dot(jnp.concatenate([x[:half], x[half:]], axis=1), mean)
    return jnp.concatenate([both[:, :wide], both[:, wide:]], axis=0)


def pair_row(ref, pair):
    return jnp.concatenate([ref[pl.ds(2 * pair, 1), :], ref[pl.ds(2 * pair + 1, 1), :]], axis=1)


def fill(whole_ref, parts, mine, rows_own):
    for rel, part in enumerate(parts):
        at = pl.multiple_of((mine ^ rel) * rows_own, rows_own)
        for g in range(part.shape[0]):
            whole_ref[pl.ds(g * len(parts) * rows_own + at, rows_own), :] = part[g]


def staggered(stages, lags, n):
    for t in range(n + max(lags)):
        for stage, lag in sorted(zip(stages, lags), key=lambda item: -item[1]):
            if 0 <= t - lag < n:
                stage(t - lag)


def activate(first, kind, slope_too):
    const = lambda x: jnp.asarray(x, kind)
    first = first.astype(kind)
    square = first * first
    inner = first * (square * const(GELU_SCALE * GELU_CUBIC) + const(GELU_SCALE))
    half = jnp.tanh(inner) * const(0.5) + const(0.5)
    active = first * half
    if not slope_too:
        return active.astype(BF)
    poly = square * const(6 * GELU_SCALE * GELU_CUBIC) + const(2 * GELU_SCALE)
    slope = half + (active - active * half) * poly
    return active.astype(BF), slope.astype(BF)


def grad_kernel(size, lags, pairs, per, lag, total, place_ref, *refs):
    key_own, value_own, key_far, value_far, rate_own, rate_far = refs[:6]
    members = (len(refs) - 15) // 2
    weight_refs = refs[6 : 6 + members]
    gain_ref, bias_ref = refs[6 + members : 8 + members]
    out_refs = refs[8 + members : 8 + 2 * members]
    whole_ref, sums_ref, active_ref, dfirst_ref, dsecond_ref, slope_ref, rate_ref = refs[-7:]
    step = pl.program_id(0)
    mine = place_ref[2]
    groups, rows_own, two = weight_refs[0].shape
    width = two // 2
    tokens = key_own.shape[0]
    heads = rate_own.shape[0]

    @pl.when(step == 0)
    def _():
        fill(whole_ref, weight_refs, mine, rows_own)
        rate_ref[...] = jnp.zeros_like(rate_ref)
        rate_ref[:tokens, :heads] = rate_own[...].T.astype(BF)
        rate_ref[tokens:, :heads] = rate_far[...].T.astype(BF)

    mean = head_mean(size, 4)
    lanes = 2 * size
    block_row = lax.broadcasted_iota(jnp.int32, (lanes + rate_ref.shape[1], 2 * lanes), 0)
    block_col = lax.broadcasted_iota(jnp.int32, (lanes + rate_ref.shape[1], 2 * lanes), 1)
    same = (block_row // size == block_col // size) & (block_row < lanes)
    zof = place_ref[0] ^ (lag[0] + lag[1] * (step * pairs // per))
    first_pair = (zof * 2 + place_ref[1]) * per + (step * pairs) % per
    const, state = [], {}
    for j in range(pairs):
        base = pl.multiple_of((step * pairs + j) * 2 * size, 2 * size)
        gain = pair_row(gain_ref, first_pair + j)
        chosen = (block_col >= lanes) & (block_row - lanes == 2 * (first_pair + j) + (block_col - lanes) // size)
        pick = jnp.where(same, 1.0 / size, jnp.where(chosen, 1.0, 0.0)).astype(BF)
        const.append((base, blocks(whole_ref[pl.ds(base, 2 * size), :], size), gain, pair_row(bias_ref, first_pair + j), gain * (1.0 / total), pick))
    sources = ((key_own, value_own), (key_far, value_far))
    starts = (first_pair * 2 * size, (zof * per + (step * pairs) % per) * 2 * size)

    def columns(far, j):
        return pl.ds(pl.multiple_of(starts[far] + j * 2 * size, 2 * size), 2 * size)

    def at(i):
        j, far = divmod(i, 2)
        return j, sources[far], columns(far, j), pl.ds(far * tokens, tokens), pl.ds(i * tokens, tokens)

    def enter(i):
        j, (key, value), cols, rows, own = at(i)
        state[i, "first"] = dot(key[:, cols], const[j][1][0]).astype(BF)

    def bend(i):
        j, (key, value), cols, rows, own = at(i)
        active, slope = activate(state.pop((i, "first")), BF, True)
        active_ref[own, :] = active
        slope_ref[own, :] = slope
        state[i, "centre"] = dot(active, const[j][1][1], NT)

    def measure(i):
        centre = state[i, "centre"]
        j, (key, value), cols, rows, own = at(i)
        both = dot(jnp.concatenate([(centre * centre).astype(BF), rate_ref[rows, :]], axis=1), const[j][5])
        state[i, "spread"], state[i, "rate"] = both[:, : 2 * size], both[:, 2 * size :]

    def compare(i):
        j, (key, value), cols, rows, own = at(i)
        _, _, gain, bias, scaled, _ = const[j]
        inverse = lax.rsqrt(state.pop((i, "spread")) + 1e-06)
        unit = state.pop((i, "centre")) * inverse
        target = value[:, cols].astype(F32) - key[:, cols].astype(F32)
        error = unit * gain + (bias - target)
        dunit = error * (state.pop((i, "rate")) * scaled)
        state[i, "along"] = averaged((dunit * unit).astype(BF), mean)
        state[i, "rest"] = (inverse, unit, dunit)

    def back(i):
        j, (key, value), cols, rows, own = at(i)
        inverse, unit, dunit = state.pop((i, "rest"))
        dsecond = (inverse * (dunit - unit * state.pop((i, "along")))).astype(BF)
        dsecond_ref[own, :] = dsecond
        state[i, "dactive"] = dot(dsecond, const[j][1][1]).astype(BF)

    def leave(i):
        j, (key, value), cols, rows, own = at(i)
        dfirst_ref[own, :] = state.pop((i, "dactive")) * slope_ref[own, :]

    def gather(i):
        j, (key, value), cols, rows, own = at(i)
        if i % 2 == 0:
            return
        base = const[j][0]
        both = pl.ds((i - 1) * tokens, 2 * tokens)
        key_t = [source[0][:, columns(far, j)].T for far, source in enumerate(sources)]
        dsecond_t = dsecond_ref[both, :].T
        for head in range(2):
            part = slice(head * size, (head + 1) * size)
            lane = slice(head * width, (head + 1) * width)
            halves = [dfirst_ref[pl.ds(k * tokens, tokens), lane] for k in (i - 1, i)]
            first = dot(key_t[0][part], halves[0]) + dot(key_t[1][part], halves[1])
            second = dot(dsecond_t[part], active_ref[both, lane])
            second = second - jnp.mean(second, axis=0, keepdims=True)
            sums_ref[pl.ds(base + head * size, size), :width] = first.astype(BF)
            sums_ref[pl.ds(base + head * size, size), width:] = second.astype(BF)

    staggered((enter, bend, measure, compare, back, leave, gather), lags, 2 * pairs)

    @pl.when(step == pl.num_programs(0) - 1)
    def _():
        for rel, out in enumerate(out_refs):
            at = pl.multiple_of((mine ^ rel) * rows_own, rows_own)
            for g in range(groups):
                out[g] = sums_ref[pl.ds(g * members * rows_own + at, rows_own), :]


def vmem(x):
    return pltpu.with_memory_space_constraint(x, pltpu.VMEM)


def gradient(place, own, far, rates, weights, gain, bias, total, lag, pairs=1, lags=(0, 1, 2, 3, 5, 6, 7)):
    tokens = own[0].shape[0]
    heads, size = gain.shape
    members = len(weights)
    groups, rows_own, two = weights[0].shape
    per = members * rows_own // (2 * size)
    held = pl.BlockSpec(memory_space=pltpu.VMEM)
    rows = groups * members * rows_own
    return pl.pallas_call(
        functools.partial(grad_kernel, size, lags, pairs, per, lag, total),
        out_shape=[pltpu.VMEM((groups, rows_own, two), BF)] * members,
        grid_spec=pltpu.PrefetchScalarGridSpec(
            num_scalar_prefetch=1,
            grid=(groups * per // pairs,),
            in_specs=[held] * (8 + members),
            out_specs=[held] * members,
            scratch_shapes=[
                pltpu.VMEM((rows, two), BF),
                pltpu.VMEM((rows, two), BF),
                pltpu.VMEM((2 * pairs * tokens, two), BF),
                pltpu.VMEM((2 * pairs * tokens, two), BF),
                pltpu.VMEM((2 * pairs * tokens, 2 * size), BF),
                pltpu.VMEM((2 * pairs * tokens, two), BF),
                pltpu.VMEM((2 * tokens, -(-heads // 128) * 128), BF),
            ],
        ),
        compiler_params=pltpu.CompilerParams(vmem_limit_bytes=40 << 20),
        name="fast_gradient",
    )(place, *map(vmem, own), *map(vmem, far), *map(vmem, rates), *map(vmem, weights), vmem(gain), vmem(bias))


def output_kernel(size, chunk, lags, lag, flip, place_ref, query_ref, weight_ref, gain_ref, bias_ref, *refs):
    out_ref, whole_ref, made_ref, sems = refs[-4:]
    members, groups, rows_own, _ = weight_ref.shape
    per = members * rows_own // (2 * size)
    fill(whole_ref, [weight_ref.at[rel] for rel in range(members)], place_ref[2], rows_own)
    mean = head_mean(size, 4)
    const, state, copies = [], {}, []
    for g in range(groups):
        first_pair = ((place_ref[0] ^ (lag[0] + lag[1] * g)) * 2 + (place_ref[1] ^ flip)) * per
        start = pl.multiple_of(first_pair * 2 * size, 2 * size)
        inside = slice(g * per * 2 * size, (g + 1) * per * 2 * size)
        copies.append(pltpu.make_async_copy(made_ref.at[:, inside], out_ref.at[:, pl.ds(start, per * 2 * size)], sems.at[g]))
        for j in range(per):
            base = (g * per + j) * 2 * size
            mats = blocks(whole_ref[pl.ds(base, 2 * size), :], size)
            column = pl.multiple_of((first_pair + j) * 2 * size, 2 * size)
            const.append((mats, pair_row(gain_ref, first_pair + j), pair_row(bias_ref, first_pair + j), column, base))
    count = query_ref.shape[0] // chunk

    def at(i):
        j, k = divmod(i, count)
        mats, gain, bias, column, base = const[j]
        rows = pl.ds(k * chunk, chunk)
        return (mats, gain, bias), (rows, pl.ds(column, 2 * size)), (rows, slice(base, base + 2 * size))

    def enter(i):
        (mats, gain, bias), where, target = at(i)
        state[i, "first"] = dot(query_ref[where], mats[0]).astype(BF)

    def bend(i):
        (mats, gain, bias), where, target = at(i)
        state[i, "centre"] = dot(activate(state.pop((i, "first")), BF, False), mats[1], NT)

    def measure(i):
        centre = state[i, "centre"]
        state[i, "spread"] = averaged((centre * centre).astype(BF), mean)

    def leave(i):
        (mats, gain, bias), where, target = at(i)
        unit = state.pop((i, "centre")) * lax.rsqrt(state.pop((i, "spread")) + 1e-06)
        made_ref[target] = (query_ref[where].astype(F32) + unit * gain + bias).astype(BF)
        if (i + 1) % (per * count) == 0:
            copies[i // (per * count)].start()

    staggered((enter, bend, measure, leave), lags, groups * per * count)
    for copy in copies:
        copy.wait()


def output(place, queries, weights, gain, bias, before, lag, flip, chunk=256, lags=(0, 1, 2, 3)):
    tokens, model = queries.shape
    members, groups, rows_own, two = weights.shape
    size = gain.shape[1]
    rows = groups * members * rows_own
    more = [] if before is None else [before]
    return pl.pallas_call(
        functools.partial(output_kernel, size, chunk, lags, lag, flip),
        out_shape=jax.ShapeDtypeStruct((tokens, model), BF),
        grid_spec=pltpu.PrefetchScalarGridSpec(
            num_scalar_prefetch=1,
            grid=(1,),
            in_specs=[pl.BlockSpec(memory_space=pltpu.VMEM)] * 4 + [pl.BlockSpec(memory_space=pl.ANY)] * len(more),
            out_specs=pl.BlockSpec(memory_space=pl.ANY),
            scratch_shapes=[
                pltpu.VMEM((rows, two), BF),
                pltpu.VMEM((tokens, rows), BF),
                pltpu.SemaphoreType.DMA((groups,)),
            ],
        ),
        input_output_aliases={5: 0} if more else {},
        compiler_params=pltpu.CompilerParams(vmem_limit_bytes=40 << 20),
        name="fast_output",
    )(place, vmem(queries), vmem(weights), vmem(gain), vmem(bias), *more)


def pick_kernel(groups, flip, place_ref, *refs):
    half = (len(refs) - 1) // 2
    sems = refs[-1]
    wide = refs[half].shape[1] // groups
    copies = []
    for k in range(half):
        for g in range(groups):
            start = pl.multiple_of((2 * g + (place_ref[1] ^ flip)) * wide, wide)
            target = refs[half + k].at[:, g * wide : (g + 1) * wide]
            copies.append(pltpu.make_async_copy(refs[k].at[:, pl.ds(start, wide)], target, sems.at[k, g]))
    for copy in copies:
        copy.start()
    for copy in copies:
        copy.wait()


def pick(place, arrays, groups, flip):
    tokens, model = arrays[0].shape
    return pl.pallas_call(
        functools.partial(pick_kernel, groups, flip),
        out_shape=[pltpu.VMEM((tokens, model // 2), a.dtype) for a in arrays],
        grid_spec=pltpu.PrefetchScalarGridSpec(
            num_scalar_prefetch=1,
            grid=(1,),
            in_specs=[pl.BlockSpec(memory_space=pltpu.HBM)] * len(arrays),
            out_specs=[pl.BlockSpec(memory_space=pltpu.VMEM)] * len(arrays),
            scratch_shapes=[pltpu.SemaphoreType.DMA((len(arrays), groups))],
        ),
        compiler_params=pltpu.CompilerParams(vmem_limit_bytes=32 << 20),
        name="pick",
    )(place, *[pltpu.with_memory_space_constraint(x, pltpu.HBM) for x in arrays])


def core_swap(x):
    n = lax.axis_size("gx")
    return lax.ppermute(x, "gx", [(i, i ^ 1) for i in range(n)])


def z_shift(x, s):
    n = lax.axis_size("gx")
    return lax.ppermute(x, "gx", [(i, i ^ (2 * s)) for i in range(n)])


def plane_shift(x, s):
    n = lax.axis_size("gy")
    return lax.ppermute(x, "gy", [(i, i ^ s) for i in range(n)])


def fetch(fast, groups, members, chunks):
    narrow = lax.optimization_barrier(fast.astype(BF))
    held = [narrow]
    for s in range(1, groups):
        held.append(z_shift(narrow, s))
    weights = []
    for at, stride in chunks:
        mine = jnp.stack([held[at + stride * g] for g in range(groups // 2)])
        weights.append([mine])
        for s in range(1, members):
            weights[-1].append(plane_shift(mine, s))
    return weights


def collect(parts, groups, members, chunks):
    sums = {}
    for part, (at, stride) in zip(parts, chunks):
        arrived = [part[0]]
        for s in range(1, members):
            arrived.append(plane_shift(part[s], s))
        for g in range(groups // 2):
            sums[at + stride * g] = sum([a[g].astype(F32) for a in arrived])
    total = sums[0]
    for s in range(1, groups):
        total = total + z_shift(sums[s].astype(BF), s).astype(F32)
    return total


def per_device(
    key_rows, value_rows, query_rows, token_rates, fast_weights, momentum, norm_gain, norm_bias
):
    size = norm_gain.shape[1]
    groups, members = lax.axis_size("gx") // 2, lax.axis_size("gy")
    total = key_rows.shape[0] * 2 * groups * members
    gx = lax.axis_index("gx")
    place = jnp.stack([gx // 2, gx % 2, lax.axis_index("gy")]).astype(jnp.int32)
    evens, odds = (0, 3), (1, 1)
    orders = [(evens, odds)] * STEPS + [((0, 1), (groups // 2, 1))]
    pairs = members * fast_weights.shape[0] // (2 * size)
    pairs = pairs if pairs <= 3 else 1
    fast, moment = (fast_weights, momentum)
    weights = fetch(fast, groups, members, orders[0])
    key_send, value_send = pick(place, (key_rows, value_rows), groups, 1)
    far = (core_swap(key_send),)
    far += (core_swap(value_send),)
    own = (key_rows, value_rows)
    rates = (token_rates.T, core_swap(token_rates).T)
    for step in range(STEPS):
        parts = []
        for k, (w, at) in enumerate(zip(weights, orders[step])):
            turn = place if k == 0 else lax.optimization_barrier((place, parts[-1][0]))[0]
            parts.append(gradient(turn, own, far, rates, w, norm_gain, norm_bias, total, at, pairs))
        grad = collect(parts, groups, members, orders[step])
        moment = momentum_keep * moment + grad
        fast = fast - inner_rate * moment
        weights = fetch(fast, groups, members, orders[step + 1])
    chunk = min(512, query_rows.shape[0])
    mixed, twins = None, []
    for w, at in zip(weights, orders[STEPS]):
        if mixed is not None:
            *w, mixed = lax.optimization_barrier((*w, mixed))
        whole = jnp.stack(w)
        twins.append(core_swap(whole))
        mixed = output(place, query_rows, whole, norm_gain, norm_bias, mixed, at, 0, chunk)
    for w, at in zip(twins, orders[STEPS]):
        mixed = output(place, query_rows, w, norm_gain, norm_bias, mixed, at, 1, chunk)
    return (mixed, fast, moment)


def plain_grad_kernel(size, chunk, total, kind, key_ref, value_ref, rate_ref, packed_ref, gain_ref, bias_ref, out_ref,
                active_ref, dfirst_ref, dsecond_ref):
    tokens = key_ref.shape[0]
    width = packed_ref.shape[1] // 2
    first_w, second_w = blocks(packed_ref[...], size)
    mean = head_mean(size, 2)
    gain = gain_ref[0]
    bias = bias_ref[0]
    scaled = gain * (1.0 / total)
    for at in range(0, tokens, chunk):
        rows = pl.ds(at, chunk)
        keys = key_ref[rows, :]
        first = dot(keys, first_w)
        active, slope = activate(first, kind, True)
        active_ref[rows, :] = active
        centre = dot(active, second_w, NT)
        spread = dot((centre * centre).astype(jnp.bfloat16), mean)
        inverse = lax.rsqrt(spread + 1e-06)
        unit = centre * inverse
        target = value_ref[rows, :].astype(jnp.float32) - keys.astype(jnp.float32)
        error = unit * gain + (bias - target)
        dunit = error * (rate_ref[rows, :].astype(jnp.float32) * scaled)
        along = dot((dunit * unit).astype(jnp.bfloat16), mean)
        dsecond = (inverse * (dunit - unit * along)).astype(jnp.bfloat16)
        dsecond_ref[rows, :] = dsecond
        dactive = dot(dsecond, second_w)
        dfirst_ref[rows, :] = (dactive * slope.astype(F32)).astype(jnp.bfloat16)
    keys_t = key_ref[...].T
    dsecond_t = dsecond_ref[...].T
    for head in range(2):
        mine = slice(head * size, (head + 1) * size)
        cols = slice(head * width, (head + 1) * width)
        out_ref[mine, :width] = dot(keys_t[mine], dfirst_ref[:, cols]).astype(out_ref.dtype)
        second = dot(dsecond_t[mine], active_ref[:, cols])
        out_ref[mine, width:] = (second - jnp.mean(second, axis=0, keepdims=True)).astype(out_ref.dtype)


def plain_apply_kernel(size, chunk, kind, query_ref, packed_ref, gain_ref, bias_ref, out_ref):
    tokens = query_ref.shape[0]
    first_w, second_w = blocks(packed_ref[...], size)
    mean = head_mean(size, 2)
    gain = gain_ref[0]
    bias = bias_ref[0]
    for at in range(0, tokens, chunk):
        rows = pl.ds(at, chunk)
        queries = query_ref[rows, :]
        first = dot(queries, first_w)
        active = activate(first, kind, False)
        centre = dot(active, second_w, NT)
        spread = dot((centre * centre).astype(jnp.bfloat16), mean)
        unit = centre * lax.rsqrt(spread + 1e-06)
        out_ref[rows, :] = (queries.astype(jnp.float32) + unit * gain + bias).astype(out_ref.dtype)


def plain_gradient(keys, values, rates, packed, gain, bias, total, size, chunk=128, kind=jnp.float32):
    tokens = keys.shape[0]
    rows, two = packed.shape
    pairs = rows // (2 * size)
    col = pl.BlockSpec((tokens, 2 * size), lambda i: (0, i))
    vec = pl.BlockSpec((1, 1, 2 * size), lambda i: (i, 0, 0))
    mat = pl.BlockSpec((2 * size, two), lambda i: (i, 0))
    return pl.pallas_call(
        functools.partial(plain_grad_kernel, size, chunk, total, kind),
        out_shape=jax.ShapeDtypeStruct((rows, two), jnp.bfloat16),
        grid=(pairs,),
        in_specs=[col, col, col, mat, vec, vec],
        out_specs=mat,
        scratch_shapes=[pltpu.VMEM((tokens, two), jnp.bfloat16), pltpu.VMEM((tokens, two), jnp.bfloat16), pltpu.VMEM((tokens, 2 * size), jnp.bfloat16)],
        name="plain_gradient",
    )(keys, values, rates, packed, gain.reshape(pairs, 1, 2 * size), bias.reshape(pairs, 1, 2 * size))


def plain_output(queries, packed, gain, bias, size, chunk=128, kind=jnp.float32):
    tokens = queries.shape[0]
    rows, two = packed.shape
    pairs = rows // (2 * size)
    col = pl.BlockSpec((tokens, 2 * size), lambda i: (0, i))
    vec = pl.BlockSpec((1, 1, 2 * size), lambda i: (i, 0, 0))
    mat = pl.BlockSpec((2 * size, two), lambda i: (i, 0))
    return pl.pallas_call(
        functools.partial(plain_apply_kernel, size, chunk, kind),
        out_shape=jax.ShapeDtypeStruct((tokens, rows), jnp.bfloat16),
        grid=(pairs,),
        in_specs=[col, mat, vec, vec],
        out_specs=col,
        name="plain_output",
    )(queries, packed, gain.reshape(pairs, 1, 2 * size), bias.reshape(pairs, 1, 2 * size))


def plain_device(
    key_rows, value_rows, query_rows, token_rates, fast_weights, momentum, norm_gain, norm_bias
):
    size = norm_gain.shape[1]
    total = key_rows.shape[0] * lax.axis_size("gx") * lax.axis_size("gy")
    place = jnp.zeros((3,), jnp.int32)
    rates = jnp.repeat(token_rates.astype(BF), size, axis=1)
    fast, moment = (fast_weights, momentum)

    def whole(fast):
        inner = lax.all_gather(fast.astype(BF), "gy", axis=0, tiled=True)
        return lax.all_gather(inner, "gx", axis=0, tiled=True)

    for _ in range(STEPS):
        part = plain_gradient(key_rows, value_rows, rates, whole(fast), norm_gain, norm_bias, total, size)
        outer = lax.psum_scatter(part, "gx", scatter_dimension=0, tiled=True)
        grad = lax.psum_scatter(outer, "gy", scatter_dimension=0, tiled=True).astype(F32)
        moment = momentum_keep * moment + grad
        fast = fast - inner_rate * moment
    mixed = plain_output(query_rows, whole(fast), norm_gain, norm_bias, size)
    return (mixed, fast, moment)


def power_of_two(n):
    return n > 0 and n & (n - 1) == 0


def solution(mesh):
    rows = P(("gx", "gy"), None)
    gx, gy = mesh.shape["gx"], mesh.shape["gy"]

    def run(*args):
        rows_own = args[0].shape[1] // mesh.size
        size = args[6].shape[1]
        paired = gx % 4 == 0 and power_of_two(gx) and power_of_two(gy)
        even = rows_own % 32 == 0 and (rows_own * gy) % (2 * size) == 0
        body = per_device if paired and even else plain_device

        return jax.shard_map(
            body,
            mesh=mesh,
            in_specs=(rows,) * 6 + (P(), P()),
            out_specs=(rows,) * 3,
            check_vma=False,
        )(*args)

    return run
```
